32 devices in a mesh: dp: 8 (over z, y), expert: 4 (over x, core).
Axes of the slice: x: 2, y: 2, z: 4, core: 2. Of those that a mesh axis runs over, the one named last changes fastest.
Arguments:
- tokens: bfloat16 [512, 2048], P(('dp', 'expert')), may hold values from -6 to 6
- expert_ids: int32 [512, 8], P(('dp', 'expert')), may hold values from 0 to 15, as said below
- route_weight: float32 [512, 8], P(('dp', 'expert')), may hold values from 0.03 to 0.6
- out_grad: bfloat16 [512, 2048], P(('dp', 'expert')), may hold values from -6 to 6
- gate_weight: bfloat16 [32, 2048, 384], P(('dp', 'expert')), may hold values from -0.125 to 0.125
- up_weight: bfloat16 [32, 2048, 384], P(('dp', 'expert')), may hold values from -0.125 to 0.125
- down_weight: bfloat16 [32, 384, 2048], P(('dp', 'expert')), may hold values from -0.21875 to 0.21875
Outputs:
- layer_out: bfloat16 [512, 2048], P(('dp', 'expert'))
- token_grad: bfloat16 [512, 2048], P(('dp', 'expert'))
- route_grad: float32 [512, 8], P(('dp', 'expert'))
- gate_grad: bfloat16 [32, 2048, 384], P(('dp', 'expert'))
- up_grad: bfloat16 [32, 2048, 384], P(('dp', 'expert'))
- down_grad: bfloat16 [32, 384, 2048], P(('dp', 'expert'))
The draws below stay inside these ranges and needn't reach their ends.
Inputs may be any that keep to these rules, and one draw needn't show every extreme that they name: `expert_ids`: each row names 8 different experts. The rows of one device name no expert more than 16 times, and one expert is named exactly 16 times by the rows of every device.
All inputs are finite; a program needn't handle non-finite values.
Results may differ from the reference program's by a relative error of at most 0.0071.
Values may be sent and summed in bfloat16 or wider, within the bound.
A program may use at most 128 MiB of HBM per device.

```python
import math
import jax
import jax.numpy as jnp
from jax import lax

D = 2048
FF = 768
TOP = 8
TOK_DEV = 16
HALF = 384
EXPERTS = 16
CAP = 16
TOKENS = 512
DEVICES = 32


def shuffle_experts(subkey):
    return jax.random.permutation(subkey, EXPERTS - 1)


def shuffle_rows(subkey):
    return jax.random.permutation(subkey, TOK_DEV)


def draw_expert_ids(key, part):
    base_key = jax.random.fold_in(key, 7)
    key_hot, key_width, key_perm, key_rows, key_turn = jax.random.split(base_key, 5)
    blocks = TOKENS // TOK_DEV
    hot_expert = jax.random.randint(key_hot, (), 0, EXPERTS)
    widths = jax.random.randint(key_width, (blocks,), EXPERTS // 2, EXPERTS)
    orders = jax.vmap(shuffle_experts)(jax.random.split(key_perm, blocks))
    others = orders + (orders >= hot_expert).astype(jnp.int32)
    row_ids = jnp.arange(TOK_DEV, dtype=jnp.int32)[:, None]
    pick_ids = jnp.arange(TOP, dtype=jnp.int32)[None, :]
    hot_slot = (row_ids < CAP) & (pick_ids == 0)
    earlier = jnp.minimum(row_ids, CAP) + ((row_ids < CAP) & (pick_ids > 0)).astype(jnp.int32)
    running = row_ids * TOP + pick_ids - earlier
    position = running[None, :, :] % widths[:, None, None]
    chosen = jnp.take_along_axis(others, position.reshape(blocks, TOK_DEV * TOP), axis=1).reshape(blocks, TOK_DEV, TOP)
    routed = jnp.where(hot_slot[None, :, :], hot_expert, chosen)
    row_perm = jax.vmap(shuffle_rows)(jax.random.split(key_rows, blocks))
    routed = jnp.take_along_axis(routed, row_perm[:, :, None], axis=1)
    rotation = jax.random.randint(key_turn, (blocks, TOK_DEV, 1), 0, TOP)
    routed = jnp.take_along_axis(routed, (pick_ids[None, :, :] + rotation) % TOP, axis=2)
    return routed.reshape(TOKENS, TOP).astype(jnp.int32)


def block_levels(key, extent, cuts, least, largest):
    gain = 1.0
    for axis_at, parts in cuts:
        heights = jax.random.uniform(jax.random.fold_in(jax.random.fold_in(key, 6), axis_at), (parts,), jnp.float32, least / len(cuts), largest / len(cuts))
        gain = gain * jnp.repeat(jnp.exp(heights), extent[axis_at] // parts).reshape((-1,) + (1,) * (len(extent) - 1 - axis_at))
    return gain


def noise(own_key, dims, deviation, limit, cuts=(), kind=jnp.bfloat16):
    entries = jax.random.normal(own_key, dims, jnp.float32) * deviation
    if len(cuts) > 0:
        entries = block_levels(own_key, dims, cuts, -0.22, 0.18) * entries
    return jnp.clip(entries, min=-limit, max=limit).astype(kind)


def setup_inputs(seed: int = 0) -> dict:
    key_of = jax.random.split(jax.random.key(seed), 8)
    tokens = noise(key_of[0], (TOKENS, D), 1.0, 6.0, ((0, 32),))
    expert_ids = draw_expert_ids(jax.random.fold_in(key_of[7], 71), 0)
    route_weight = jnp.clip(jnp.exp(math.log(0.6) - 2.9957323 * jax.random.uniform(key_of[2], (TOKENS, TOP), jnp.float32) ** block_levels(key_of[2], (TOKENS, TOP), ((0, 32),), -0.2, 0.2)), 0.03, 0.6)
    out_grad = noise(key_of[3], (TOKENS, D), 1.0, 6.0, ((0, 32),))
    gate_weight = noise(key_of[4], (DEVICES, D, HALF), D ** -0.5, 0.125, ((0, 32),))
    up_weight = noise(key_of[5], (DEVICES, D, HALF), D ** -0.5, 0.125, ((0, 32),))
    down_weight = noise(key_of[6], (DEVICES, HALF, D), FF ** -0.5, 0.21875, ((0, 32),))
    return dict(tokens=tokens, expert_ids=expert_ids, route_weight=route_weight, out_grad=out_grad, gate_weight=gate_weight, up_weight=up_weight, down_weight=down_weight)


def reference(tokens, expert_ids, route_weight, out_grad, gate_weight, up_weight, down_weight):
    tok_total = tokens.shape[0]
    assigned = tok_total * TOP
    flat_ids = expert_ids.reshape(-1).astype(jnp.int32)
    per_block = flat_ids.reshape(-1, TOK_DEV * TOP)
    onehot = (per_block[:, :, None] == jnp.arange(EXPERTS, dtype=jnp.int32)[None, None, :]).astype(jnp.int32)
    before = jnp.cumsum(onehot, axis=1) - onehot
    slot_ids = jnp.sum(before * onehot, axis=2).reshape(-1).astype(jnp.int32)
    device_ids = jnp.arange(assigned, dtype=jnp.int32) // (TOK_DEV * TOP)
    place_row = ((flat_ids * DEVICES + device_ids) * CAP + slot_ids).astype(jnp.int32)
    slot_table = jnp.full((EXPERTS * DEVICES * CAP,), -1, jnp.int32).at[place_row].set(jnp.arange(assigned, dtype=jnp.int32))
    slot_table = slot_table.reshape(EXPERTS, DEVICES * CAP)
    weights_flat = route_weight.reshape(-1)

    def expert_step(accum, expert):
        out_acc, grad_acc, route_acc = accum
        entry_ids = slot_table[expert]
        filled = entry_ids >= 0
        assign = jnp.maximum(entry_ids, 0)
        tok_rows = assign // TOP
        in_rows = jnp.where(filled[:, None], tokens[tok_rows], jnp.zeros((), jnp.bfloat16))
        weight_rows = jnp.where(filled, weights_flat[assign], jnp.zeros((), jnp.float32))
        grad_rows = out_grad[tok_rows].astype(jnp.float32)
        scaled = (weight_rows[:, None] * grad_rows).astype(jnp.bfloat16)
        partials = []
        partial_grads = []
        gate_pieces = []
        up_pieces = []
        down_pieces = []
        for piece_half in range(2):
            piece_id = 2 * expert + piece_half
            w_gate = gate_weight[piece_id]
            w_up = up_weight[piece_id]
            w_down = down_weight[piece_id]
            gate_act = jnp.dot(in_rows, w_gate, preferred_element_type=jnp.float32)
            up_act = jnp.dot(in_rows, w_up, preferred_element_type=jnp.float32)
            sig_gate = jax.nn.sigmoid(gate_act)
            hidden = (gate_act * sig_gate * up_act).astype(jnp.bfloat16)
            partials.append(jnp.dot(hidden, w_down, preferred_element_type=jnp.float32).astype(jnp.bfloat16))
            hidden_grad = jnp.dot(scaled, w_down.T, preferred_element_type=jnp.float32)
            gate_pre = (hidden_grad * up_act * sig_gate * (1.0 + gate_act * (1.0 - sig_gate))).astype(jnp.bfloat16)
            up_pre = (hidden_grad * gate_act * sig_gate).astype(jnp.bfloat16)
            partial_grads.append((jnp.dot(gate_pre, w_gate.T, preferred_element_type=jnp.float32) + jnp.dot(up_pre, w_up.T, preferred_element_type=jnp.float32)).astype(jnp.bfloat16))
            gate_pieces.append(jnp.dot(in_rows.T, gate_pre, preferred_element_type=jnp.float32).astype(jnp.bfloat16))
            up_pieces.append(jnp.dot(in_rows.T, up_pre, preferred_element_type=jnp.float32).astype(jnp.bfloat16))
            down_pieces.append(jnp.dot(hidden.T, scaled, preferred_element_type=jnp.float32).astype(jnp.bfloat16))
        expert_out = (partials[0].astype(jnp.float32) + partials[1].astype(jnp.float32)).astype(jnp.bfloat16)
        out_acc = out_acc.at[tok_rows].add(weight_rows[:, None] * expert_out.astype(jnp.float32))
        route_term = jnp.sum(grad_rows * expert_out.astype(jnp.float32), axis=1)
        route_acc = route_acc.at[assign].add(jnp.where(filled, route_term, jnp.zeros((), jnp.float32)))
        expert_grad = (partial_grads[0].astype(jnp.float32) + partial_grads[1].astype(jnp.float32)).astype(jnp.bfloat16)
        grad_acc = grad_acc.at[tok_rows].add(jnp.where(filled[:, None], expert_grad.astype(jnp.float32), jnp.zeros((), jnp.float32)))
        return (out_acc, grad_acc, route_acc), (jnp.stack(gate_pieces), jnp.stack(up_pieces), jnp.stack(down_pieces))

    start = (jnp.zeros((tok_total, D), jnp.float32), jnp.zeros((tok_total, D), jnp.float32), jnp.zeros((assigned,), jnp.float32))
    final, stacked = lax.scan(expert_step, start, jnp.arange(EXPERTS, dtype=jnp.int32))
    out_acc, grad_acc, route_acc = final
    gate_all, up_all, down_all = stacked
    return (out_acc.astype(jnp.bfloat16), grad_acc.astype(jnp.bfloat16), route_acc.reshape(tok_total, TOP),
            gate_all.reshape(DEVICES, D, HALF), up_all.reshape(DEVICES, D, HALF), down_all.reshape(DEVICES, HALF, D))
```

```python
import jax
import jax.numpy as jnp
from jax import lax
from jax.sharding import PartitionSpec as P


def from_partner(shard, axis, apart):
    return lax.ppermute(shard, axis, [(i, i ^ 1 << apart) for i in range(lax.axis_size(axis))])


def contract(left_op, right_op, left_dim, right_dim):
    return lax.dot_general(
        left_op,
        right_op,
        (((left_dim,), (right_dim,)), ((), ())),
        preferred_element_type=jnp.float32,
    )


def deliver(buffer, dp_size, ex_size, experts, capacity, backward):
    feat_width = buffer.shape[1]
    doubled = jnp.broadcast_to(
        buffer.reshape(experts, 1, capacity, feat_width), (experts, 2, capacity, feat_width)
    )
    doubled = doubled.reshape(dp_size, ex_size, capacity, feat_width)
    if backward:
        arrived = lax.all_to_all(
            lax.all_to_all(doubled, "dp", split_axis=0, concat_axis=0, tiled=True),
            "expert",
            split_axis=1,
            concat_axis=1,
            tiled=True,
        )
    else:
        arrived = lax.all_to_all(
            lax.all_to_all(doubled, "dp", split_axis=0, concat_axis=0, tiled=True),
            "expert",
            split_axis=1,
            concat_axis=1,
            tiled=True,
        )
    return arrived.reshape(-1, feat_width)


def bring_back(partials_in, dp_size, ex_size, experts, capacity, half_index, backward):
    feat_width = partials_in.shape[1]
    if backward:
        partner = from_partner(partials_in, "expert", 0)
    else:
        partner = from_partner(partials_in, "expert", 0)
    summed = (partials_in.astype(jnp.float32) + partner.astype(jnp.float32)).astype(jnp.bfloat16)
    summed = summed.reshape(dp_size, ex_size, capacity, feat_width)
    own_half = lax.dynamic_slice_in_dim(summed, half_index * (capacity // 2), capacity // 2, 2)
    if backward:
        returned = lax.all_to_all(
            lax.all_to_all(own_half, "dp", split_axis=0, concat_axis=0, tiled=True),
            "expert",
            split_axis=1,
            concat_axis=1,
            tiled=True,
        )
    else:
        returned = lax.all_to_all(
            lax.all_to_all(own_half, "dp", split_axis=0, concat_axis=0, tiled=True),
            "expert",
            split_axis=1,
            concat_axis=1,
            tiled=True,
        )
    merged = returned.reshape(experts, capacity, feat_width)
    return merged.reshape(experts * capacity, feat_width)


AXES = ("dp", "expert")


def dense_body(tokens, expert_ids, route_weight, out_grad, gate_weight, up_weight, down_weight):
    pieces = lax.axis_size("dp") * lax.axis_size("expert")
    experts = pieces // 2
    tok_count, feat_width = tokens.shape
    mine = (lax.axis_index("dp") * lax.axis_size("expert") + lax.axis_index("expert")) // 2
    onehot = expert_ids[:, :, None] == jnp.arange(experts, dtype=jnp.int32)
    table = jnp.sum(jnp.where(onehot, route_weight[:, :, None], 0.0), axis=1)
    both = lax.all_gather(jnp.concatenate([tokens, out_grad], axis=1), AXES, axis=0, tiled=True)
    x_all, g_all = both[:, :feat_width], both[:, feat_width:]
    weights = lax.all_gather(table, AXES, axis=0, tiled=True)
    weight = lax.dynamic_slice_in_dim(weights, mine, 1, 1)
    w_gate, w_up, w_down = gate_weight[0], up_weight[0], down_weight[0]
    gate_act = contract(x_all, w_gate, 1, 0)
    up_act = contract(x_all, w_up, 1, 0)
    back = contract(g_all, w_down, 1, 1)
    sig = jax.nn.sigmoid(gate_act)
    hidden = gate_act * sig * up_act
    route = jnp.sum(hidden * back, axis=1)
    scaled_hidden = (weight * hidden).astype(jnp.bfloat16)
    back = weight * back
    gate_pre = (back * up_act * sig * (1.0 + gate_act * (1.0 - sig))).astype(jnp.bfloat16)
    up_pre = (back * gate_act * sig).astype(jnp.bfloat16)
    out_part = contract(scaled_hidden, w_down, 1, 0).astype(jnp.bfloat16)
    grad_part = (contract(gate_pre, w_gate, 1, 1) + contract(up_pre, w_up, 1, 1)).astype(
        jnp.bfloat16
    )
    gate_grad = contract(x_all, gate_pre, 0, 0).astype(jnp.bfloat16)
    up_grad = contract(x_all, up_pre, 0, 0).astype(jnp.bfloat16)
    down_grad = contract(scaled_hidden, g_all, 0, 0).astype(jnp.bfloat16)
    summed = lax.psum_scatter(
        jnp.concatenate([out_part, grad_part], axis=1), AXES, scatter_dimension=0, tiled=True
    )
    routes = lax.all_to_all(route.reshape(pieces, tok_count), AXES, 0, 0, tiled=True)
    routes = jnp.sum(routes.reshape(experts, 2, tok_count), axis=1)
    route_grad = jnp.sum(jnp.where(onehot, routes.T[:, None, :], 0.0), axis=2)
    return (
        summed[:, :feat_width],
        summed[:, feat_width:],
        route_grad,
        gate_grad[None],
        up_grad[None],
        down_grad[None],
    )


def body(tokens, expert_ids, route_weight, out_grad, gate_weight, up_weight, down_weight):
    dp_size = lax.axis_size("dp")
    ex_size = lax.axis_size("expert")
    tok_count, feat_width = tokens.shape
    top_count = expert_ids.shape[1]
    experts = dp_size * ex_size // 2
    assigned = tok_count * top_count
    capacity = 2 * (assigned // experts)
    half_index = lax.axis_index("expert") % 2
    flat_ids = expert_ids.reshape(-1)
    onehot = (flat_ids[:, None] == jnp.arange(experts, dtype=jnp.int32)[None, :]).astype(jnp.int32)
    before = jnp.cumsum(onehot, axis=0) - onehot
    slot_ids = jnp.sum(before * onehot, axis=1)
    place_row = flat_ids * capacity + slot_ids
    source = (
        jnp.full((experts * capacity,), -1, jnp.int32)
        .at[place_row]
        .set(jnp.arange(assigned, dtype=jnp.int32))
    )
    filled = source >= 0
    assign = jnp.maximum(source, 0)
    rows_tok = assign // top_count
    send_rows = jnp.where(filled[:, None], tokens[rows_tok], jnp.zeros((), jnp.bfloat16))
    in_rows = deliver(send_rows, dp_size, ex_size, experts, capacity, False)
    w_gate = gate_weight[0]
    w_up = up_weight[0]
    w_down = down_weight[0]
    gate_act = jnp.dot(in_rows, w_gate, preferred_element_type=jnp.float32)
    up_act = jnp.dot(in_rows, w_up, preferred_element_type=jnp.float32)
    sig_gate = jax.nn.sigmoid(gate_act)
    hidden = (gate_act * sig_gate * up_act).astype(jnp.bfloat16)
    partial_value = jnp.dot(hidden, w_down, preferred_element_type=jnp.float32).astype(jnp.bfloat16)
    expert_table = bring_back(partial_value, dp_size, ex_size, experts, capacity, half_index, False)
    expert_rows = expert_table[place_row].reshape(tok_count, top_count, feat_width)
    layer_out = jnp.sum(route_weight[:, :, None] * expert_rows.astype(jnp.float32), axis=1).astype(
        jnp.bfloat16
    )
    route_grad = jnp.einsum("tkd,td->tk", expert_rows, out_grad, preferred_element_type=jnp.float32)
    scaled = (route_weight[:, :, None] * out_grad[:, None, :].astype(jnp.float32)).astype(
        jnp.bfloat16
    )
    scaled = scaled.reshape(assigned, feat_width)
    send_grad = jnp.where(filled[:, None], scaled[assign], jnp.zeros((), jnp.bfloat16))
    grad_rows = deliver(send_grad, dp_size, ex_size, experts, capacity, True)
    hidden_grad = contract(grad_rows, w_down, 1, 1)
    gate_pre = (hidden_grad * up_act * sig_gate * (1.0 + gate_act * (1.0 - sig_gate))).astype(
        jnp.bfloat16
    )
    up_pre = (hidden_grad * gate_act * sig_gate).astype(jnp.bfloat16)
    partial_grad = (contract(gate_pre, w_gate, 1, 1) + contract(up_pre, w_up, 1, 1)).astype(
        jnp.bfloat16
    )
    gate_grad = contract(in_rows, gate_pre, 0, 0).astype(jnp.bfloat16)
    up_grad = contract(in_rows, up_pre, 0, 0).astype(jnp.bfloat16)
    down_grad = contract(hidden, grad_rows, 0, 0).astype(jnp.bfloat16)
    grad_table = bring_back(partial_grad, dp_size, ex_size, experts, capacity, half_index, True)
    expert_grad = grad_table[place_row].reshape(tok_count, top_count, feat_width)
    token_grad = jnp.sum(expert_grad.astype(jnp.float32), axis=1).astype(jnp.bfloat16)
    return (layer_out, token_grad, route_grad, gate_grad[None], up_grad[None], down_grad[None])


def solution(mesh):
    in_specs = (
        P(("dp", "expert"), None),
        P(("dp", "expert"), None),
        P(("dp", "expert"), None),
        P(("dp", "expert"), None),
        P(("dp", "expert"), None, None),
        P(("dp", "expert"), None, None),
        P(("dp", "expert"), None, None),
    )
    out_specs = (
        P(("dp", "expert"), None),
        P(("dp", "expert"), None),
        P(("dp", "expert"), None),
        P(("dp", "expert"), None, None),
        P(("dp", "expert"), None, None),
        P(("dp", "expert"), None, None),
    )
    pieces = mesh.shape["dp"] * mesh.shape["expert"]

    def step(tokens, expert_ids, *rest):
        capacity = 2 * (tokens.shape[0] * expert_ids.shape[1] // (pieces // 2))
        form = dense_body if capacity >= tokens.shape[0] else body
        return form(tokens, expert_ids, *rest)

    return jax.shard_map(step, mesh=mesh, in_specs=in_specs, out_specs=out_specs, check_vma=False)
```

```python
import functools

import jax
import jax.numpy as jnp
from jax import lax
from jax.experimental import pallas as pl
from jax.experimental.pallas import tpu as pltpu
from jax.sharding import PartitionSpec as P

LANES = 128
TILE = 256


def from_partner(shard, axis, apart):
    return lax.ppermute(shard, axis, [(i, i ^ 1 << apart) for i in range(lax.axis_size(axis))])


def contract(left_op, right_op, left_dim, right_dim):
    return lax.dot_general(
        left_op,
        right_op,
        (((left_dim,), (right_dim,)), ((), ())),
        preferred_element_type=jnp.float32,
    )


def deliver(buffer, dp_size, ex_size, experts, capacity, backward):
    feat_width = buffer.shape[1]
    doubled = jnp.broadcast_to(
        buffer.reshape(experts, 1, capacity, feat_width), (experts, 2, capacity, feat_width)
    )
    doubled = doubled.reshape(dp_size, ex_size, capacity, feat_width)
    if backward:
        arrived = lax.all_to_all(
            lax.all_to_all(doubled, "dp", split_axis=0, concat_axis=0, tiled=True),
            "expert",
            split_axis=1,
            concat_axis=1,
            tiled=True,
        )
    else:
        arrived = lax.all_to_all(
            lax.all_to_all(doubled, "dp", split_axis=0, concat_axis=0, tiled=True),
            "expert",
            split_axis=1,
            concat_axis=1,
            tiled=True,
        )
    return arrived.reshape(-1, feat_width)


def bring_back(partials_in, dp_size, ex_size, experts, capacity, half_index, backward):
    feat_width = partials_in.shape[1]
    if backward:
        partner = from_partner(partials_in, "expert", 0)
    else:
        partner = from_partner(partials_in, "expert", 0)
    summed = (partials_in.astype(jnp.float32) + partner.astype(jnp.float32)).astype(jnp.bfloat16)
    summed = summed.reshape(dp_size, ex_size, capacity, feat_width)
    own_half = lax.dynamic_slice_in_dim(summed, half_index * (capacity // 2), capacity // 2, 2)
    if backward:
        returned = lax.all_to_all(
            lax.all_to_all(own_half, "dp", split_axis=0, concat_axis=0, tiled=True),
            "expert",
            split_axis=1,
            concat_axis=1,
            tiled=True,
        )
    else:
        returned = lax.all_to_all(
            lax.all_to_all(own_half, "dp", split_axis=0, concat_axis=0, tiled=True),
            "expert",
            split_axis=1,
            concat_axis=1,
            tiled=True,
        )
    merged = returned.reshape(experts, capacity, feat_width)
    return merged.reshape(experts * capacity, feat_width)


def body(tokens, expert_ids, route_weight, out_grad, gate_weight, up_weight, down_weight):
    dp_size = lax.axis_size("dp")
    ex_size = lax.axis_size("expert")
    tok_count, feat_width = tokens.shape
    top_count = expert_ids.shape[1]
    experts = dp_size * ex_size // 2
    assigned = tok_count * top_count
    capacity = 2 * (assigned // experts)
    half_index = lax.axis_index("expert") % 2
    flat_ids = expert_ids.reshape(-1)
    onehot = (flat_ids[:, None] == jnp.arange(experts, dtype=jnp.int32)[None, :]).astype(jnp.int32)
    before = jnp.cumsum(onehot, axis=0) - onehot
    slot_ids = jnp.sum(before * onehot, axis=1)
    place_row = flat_ids * capacity + slot_ids
    source = (
        jnp.full((experts * capacity,), -1, jnp.int32)
        .at[place_row]
        .set(jnp.arange(assigned, dtype=jnp.int32))
    )
    filled = source >= 0
    assign = jnp.maximum(source, 0)
    rows_tok = assign // top_count
    send_rows = jnp.where(filled[:, None], tokens[rows_tok], jnp.zeros((), jnp.bfloat16))
    in_rows = deliver(send_rows, dp_size, ex_size, experts, capacity, False)
    w_gate = gate_weight[0]
    w_up = up_weight[0]
    w_down = down_weight[0]
    gate_act = jnp.dot(in_rows, w_gate, preferred_element_type=jnp.float32)
    up_act = jnp.dot(in_rows, w_up, preferred_element_type=jnp.float32)
    sig_gate = jax.nn.sigmoid(gate_act)
    hidden = (gate_act * sig_gate * up_act).astype(jnp.bfloat16)
    partial_value = jnp.dot(hidden, w_down, preferred_element_type=jnp.float32).astype(jnp.bfloat16)
    expert_table = bring_back(partial_value, dp_size, ex_size, experts, capacity, half_index, False)
    expert_rows = expert_table[place_row].reshape(tok_count, top_count, feat_width)
    layer_out = jnp.sum(route_weight[:, :, None] * expert_rows.astype(jnp.float32), axis=1).astype(
        jnp.bfloat16
    )
    route_grad = jnp.einsum("tkd,td->tk", expert_rows, out_grad, preferred_element_type=jnp.float32)
    scaled = (route_weight[:, :, None] * out_grad[:, None, :].astype(jnp.float32)).astype(
        jnp.bfloat16
    )
    scaled = scaled.reshape(assigned, feat_width)
    send_grad = jnp.where(filled[:, None], scaled[assign], jnp.zeros((), jnp.bfloat16))
    grad_rows = deliver(send_grad, dp_size, ex_size, experts, capacity, True)
    hidden_grad = contract(grad_rows, w_down, 1, 1)
    gate_pre = (hidden_grad * up_act * sig_gate * (1.0 + gate_act * (1.0 - sig_gate))).astype(
        jnp.bfloat16
    )
    up_pre = (hidden_grad * gate_act * sig_gate).astype(jnp.bfloat16)
    partial_grad = (contract(gate_pre, w_gate, 1, 1) + contract(up_pre, w_up, 1, 1)).astype(
        jnp.bfloat16
    )
    gate_grad = contract(in_rows, gate_pre, 0, 0).astype(jnp.bfloat16)
    up_grad = contract(in_rows, up_pre, 0, 0).astype(jnp.bfloat16)
    down_grad = contract(hidden, grad_rows, 0, 0).astype(jnp.bfloat16)
    grad_table = bring_back(partial_grad, dp_size, ex_size, experts, capacity, half_index, True)
    expert_grad = grad_table[place_row].reshape(tok_count, top_count, feat_width)
    token_grad = jnp.sum(expert_grad.astype(jnp.float32), axis=1).astype(jnp.bfloat16)
    return (layer_out, token_grad, route_grad, gate_grad[None], up_grad[None], down_grad[None])


def expert_kernel(
    planes, tok_count, width, half, experts, tile,
    tok_ref, ids_ref, rw_ref, og_ref, wg_hbm, wu_hbm, wd_hbm,
    lo_ref, tg_ref, rg_ref, gg_ref, ug_ref, dg_ref,
    rows, parts, swapped, summed, first_a, first_b, turn_a, turn_b, second_a, second_b,
    zsend, zrecv, zown, hidden_all, pre_all, wg_ref, wu_ref, wd_ref,
    load_sem, z_ss, z_rs, x_ss, x_rs, y_ss, y_rs, xh_ss, xh_rs, yh_ss, yh_rs,
    core_ss, core_rs, swap_ss, swap_rs, fa_ss, fa_rs, fb_ss, fb_rs,
    ta_ss, ta_rs, tb_ss, tb_rs, zo_ss, zo_rs,
):
    f32, bf16 = jnp.float32, jnp.bfloat16
    dp, ex = lax.axis_index("dp"), lax.axis_index("expert")
    z, y, x, c = dp // 2, dp % 2, ex // 2, ex % 2
    piece = dp * lax.axis_size("expert") + ex
    mine = piece // 2
    full = 2 * width + LANES
    x_dev, y_dev, core_dev = (dp, (1 - x) * 2 + c), (z * 2 + 1 - y, ex), (dp, x * 2 + 1 - c)
    here, over_x, over_y, over_xy = y * 2 + x, y * 2 + 1 - x, (1 - y) * 2 + x, (1 - y) * 2 + 1 - x
    left, right = pl.ds(0, width), pl.ds(width, width + LANES)

    def remote(src, dst, send, recv, device):
        return pltpu.make_async_remote_copy(
            src_ref=src, dst_ref=dst, send_sem=send, recv_sem=recv,
            device_id=device, device_id_type=pl.DeviceIdType.MESH,
        )

    def landed(dst, send, recv):
        remote(dst, dst, send, recv, core_dev).wait_recv()

    def plane(step):
        return (z + planes - step) % planes

    def load(i):
        src = (wg_hbm, wu_hbm, wd_hbm)[i]
        dst = (wg_ref, wu_ref, wd_ref)[i]
        return pltpu.make_async_copy(src.at[0], dst, load_sem.at[i])

    for i in range(3):
        load(i).start()

    lane = lax.broadcasted_iota(jnp.int32, (tok_count, LANES), 1)
    ids, weights = ids_ref[...], rw_ref[...]
    table = [jnp.zeros((tok_count, LANES), f32) for _ in range(3)]
    for k in range(ids.shape[1]):
        for part in range(3):
            hit = lane == ids[:, k : k + 1] + part * experts
            table[part] = jnp.where(hit, weights[:, k : k + 1], table[part])
    head = table[0].astype(bf16).astype(f32)
    mid = table[1] - table[1].astype(bf16).astype(f32)
    mid = mid.astype(bf16).astype(f32)
    rest = table[2] - table[2].astype(bf16).astype(f32)
    rest = rest - rest.astype(bf16).astype(f32)
    rows[z, c, here, :, pl.ds(0, width)] = tok_ref[...]
    rows[z, c, here, :, pl.ds(width, width)] = og_ref[...]
    rows[z, c, here, :, pl.ds(2 * width, LANES)] = (head + mid + rest).astype(bf16)

    barrier = pltpu.get_barrier_semaphore()
    peers = [x_dev, y_dev, core_dev]
    peers += [(((z + d) % planes) * 2 + y, ex) for d in range(1, planes)]
    for peer in peers:
        pl.semaphore_signal(barrier, inc=1, device_id=peer, device_id_type=pl.DeviceIdType.MESH)
    pl.semaphore_wait(barrier, len(peers))

    def z_copy(d):
        slot = rows.at[z, c, here]
        peer = (((z + d) % planes) * 2 + y, ex)
        return remote(slot, slot, z_ss.at[d - 1], z_rs.at[d - 1], peer)

    def x_copy(s):
        slot = rows.at[plane(s), c, here]
        return remote(slot, slot, x_ss.at[s], x_rs.at[s], x_dev)

    def y_copy(s):
        slot = rows.at[plane(s), c, here]
        return remote(slot, slot, y_ss.at[s], y_rs.at[s], y_dev)

    def xh_copy(s):
        slot = rows.at[plane(s), c, over_y, :, left]
        return remote(slot, slot, xh_ss.at[s], xh_rs.at[s], x_dev)

    def yh_copy(s):
        slot = rows.at[plane(s), c, over_x, :, right]
        return remote(slot, slot, yh_ss.at[s], yh_rs.at[s], y_dev)

    def core_copy(s, which):
        slot = rows.at[plane(s), c, (here, over_x, over_y, over_xy)[which]]
        return remote(slot, slot, core_ss.at[s, which], core_rs.at[s, which], core_dev)

    def swap_copy(s):
        q = plane(s)
        return remote(parts.at[q, 1 - c], swapped.at[q], swap_ss.at[s], swap_rs.at[s], core_dev)

    def fa_copy(s, to_y):
        src = summed.at[plane(s), to_y * 2 + 1 - x, :, left]
        return remote(src, first_a.at[s, to_y], fa_ss.at[s, to_y], fa_rs.at[s, to_y], x_dev)

    def fb_copy(s, to_x):
        src = summed.at[plane(s), (1 - y) * 2 + to_x, :, right]
        return remote(src, first_b.at[s, to_x], fb_ss.at[s, to_x], fb_rs.at[s, to_x], y_dev)

    def ta_copy(s):
        return remote(turn_a.at[s], second_a.at[s], ta_ss.at[s], ta_rs.at[s], y_dev)

    def tb_copy(s):
        return remote(turn_b.at[s], second_b.at[s], tb_ss.at[s], tb_rs.at[s], x_dev)

    def zo_copy(s):
        peer = (plane(s) * 2 + y, ex)
        return remote(zsend.at[s - 1], zrecv.at[s - 1], zo_ss.at[s - 1], zo_rs.at[s - 1], peer)

    def gather_one(s):
        @pl.when(s > 0)
        def _():
            landed(rows.at[plane(s), c, here], z_ss.at[s - 1], z_rs.at[s - 1])

        x_copy(s).start()
        y_copy(s).start()
        core_copy(s, 0).start()

    def gather_two(s):
        q = plane(s)
        landed(rows.at[q, c, over_x], x_ss.at[s], x_rs.at[s])
        yh_copy(s).start()
        core_copy(s, 1).start()
        landed(rows.at[q, c, over_y], y_ss.at[s], y_rs.at[s])
        xh_copy(s).start()
        core_copy(s, 2).start()

    def gather_three(s):
        q = plane(s)
        landed(rows.at[q, c, over_xy, :, left], xh_ss.at[s], xh_rs.at[s])
        landed(rows.at[q, c, over_xy, :, right], yh_ss.at[s], yh_rs.at[s])
        core_copy(s, 3).start()

    group = 8 * tok_count
    glane = lax.broadcasted_iota(jnp.int32, (group, LANES), 1)

    def compute(s):
        q = plane(s)
        for which, slot in enumerate((here, over_x, over_y, over_xy)):
            landed(rows.at[q, 1 - c, slot], core_ss.at[s, which], core_rs.at[s, which])
        x_in = rows[q, :, :, :, 0:width].reshape(group, width)
        g_in = rows[q, :, :, :, width : 2 * width].reshape(group, width)
        gate = contract(x_in, wg_ref[...], 1, 0)
        up = contract(x_in, wu_ref[...], 1, 0)
        back = contract(g_in, wd_ref[...], 1, 1)
        tab = rows[q, :, :, :, 2 * width : full].reshape(group, LANES).astype(f32)
        own = (glane == mine) | (glane == mine + experts) | (glane == mine + 2 * experts)
        weight = jnp.sum(jnp.where(own, tab, 0.0), axis=1, keepdims=True)
        sig = 1.0 / (1.0 + jnp.exp(-gate))
        act = gate * sig
        hidden = act * up
        route = jnp.sum(hidden * back, axis=1, keepdims=True)
        coarse = route.astype(bf16).astype(f32)
        fine = route - coarse
        marks = jnp.where(glane == piece, coarse, jnp.where(glane == piece + LANES // 2, fine, 0.0))
        back = weight * back
        hid = (weight * hidden).astype(bf16)
        gate_pre = (back * up * sig * (1.0 + gate * (1.0 - sig))).astype(bf16)
        up_pre = (back * act).astype(bf16)
        at = pl.ds(pl.multiple_of(q * group, group), group)
        hidden_all[at, :] = hid
        pre_all[at, 0:half] = gate_pre
        pre_all[at, half : 2 * half] = up_pre
        shape = (2, 4, tok_count)
        for n in range(0, width, 2 * tile):
            cols = slice(n, n + 2 * tile)
            out = contract(hid, wd_ref[:, cols], 1, 0)
            parts[q, :, :, :, cols] = out.astype(bf16).reshape(shape + (2 * tile,))
            grad = contract(gate_pre, wg_ref[cols, :], 1, 1) + contract(up_pre, wu_ref[cols, :], 1, 1)
            after = slice(width + n, width + n + 2 * tile)
            parts[q, :, :, :, after] = grad.astype(bf16).reshape(shape + (2 * tile,))
        parts[q, :, :, :, 2 * width : full] = marks.astype(bf16).reshape(shape + (LANES,))
        swap_copy(s).start()

    def reduce_one(s):
        q = plane(s)
        landed(swapped.at[q], swap_ss.at[s], swap_rs.at[s])

        def add(t, carry):
            total = parts[q, c, t].astype(f32) + swapped[q, t].astype(f32)
            summed[q, t] = total.astype(bf16)
            return carry

        lax.fori_loop(0, 4, add, 0)
        fa_copy(s, 1 - y).start()
        fb_copy(s, 1 - x).start()
        fa_copy(s, y).start()
        fb_copy(s, x).start()

    def reduce_two(s):
        q = plane(s)
        landed(first_a.at[s, 1 - y], fa_ss.at[s, 1 - y], fa_rs.at[s, 1 - y])
        total = summed[q, over_y, :, 0:width].astype(f32) + first_a[s, 1 - y].astype(f32)
        turn_a[s] = total.astype(bf16)
        ta_copy(s).start()
        landed(first_b.at[s, 1 - x], fb_ss.at[s, 1 - x], fb_rs.at[s, 1 - x])
        total = summed[q, over_x, :, width:full].astype(f32) + first_b[s, 1 - x].astype(f32)
        turn_b[s] = total.astype(bf16)
        tb_copy(s).start()

    def reduce_three(s):
        q = plane(s)
        landed(first_a.at[s, y], fa_ss.at[s, y], fa_rs.at[s, y])
        landed(first_b.at[s, x], fb_ss.at[s, x], fb_rs.at[s, x])
        landed(second_a.at[s], ta_ss.at[s], ta_rs.at[s])
        landed(second_b.at[s], tb_ss.at[s], tb_rs.at[s])
        total_a = summed[q, here, :, 0:width].astype(f32) + first_a[s, y].astype(f32)
        total_a = total_a + second_a[s].astype(f32)
        total_b = summed[q, here, :, width:full].astype(f32) + first_b[s, x].astype(f32)
        total_b = total_b + second_b[s].astype(f32)

        @pl.when(s == 0)
        def _():
            zown[:, 0:width] = total_a
            zown[:, width:full] = total_b

        @pl.when(s > 0)
        def _():
            zsend[s - 1, :, 0:width] = total_a.astype(bf16)
            zsend[s - 1, :, width:full] = total_b.astype(bf16)
            zo_copy(s).start()

    every = planes * group
    tiles = width // tile

    def weight_grads(t, carry):
        cols = pl.ds(pl.multiple_of(t * tile, tile), tile)
        x_in = rows[:, :, :, :, cols].reshape(every, tile)
        after = pl.ds(pl.multiple_of(width + t * tile, tile), tile)
        g_in = rows[:, :, :, :, after].reshape(every, tile)
        both = contract(x_in, pre_all[...], 0, 0).astype(bf16)
        gg_ref[0, cols, :] = both[:, 0:half]
        ug_ref[0, cols, :] = both[:, half : 2 * half]
        dg_ref[0, :, cols] = contract(hidden_all[...], g_in, 0, 0).astype(bf16)
        return carry

    for d in range(1, planes):
        z_copy(d).start()

    def step(i, carry):
        def stage(at, run):
            @pl.when((i >= at) & (i < at + planes))
            def _():
                run(i - at)

        stage(0, gather_one)
        stage(1, gather_two)
        stage(2, gather_three)

        @pl.when(i == 3)
        def _():
            for j in range(3):
                load(j).wait()

        stage(3, compute)
        stage(4, reduce_one)
        stage(5, reduce_two)
        stage(6, reduce_three)

        @pl.when(i >= planes + 3)
        def _():
            j = i - (planes + 3)
            lax.fori_loop((j * tiles) // 3, ((j + 1) * tiles) // 3, weight_grads, 0)

        return carry

    lax.fori_loop(0, planes + 6, step, 0)

    total = zown[...]
    for s in range(1, planes):
        landed(zrecv.at[s - 1], zo_ss.at[s - 1], zo_rs.at[s - 1])
        total = total + zrecv[s - 1].astype(f32)
    lo_ref[...] = total[:, 0:width].astype(bf16)
    tg_ref[...] = total[:, width : 2 * width].astype(bf16)
    marks = total[:, 2 * width : full]
    routes = jnp.zeros((tok_count, LANES), f32)
    for k in range(ids.shape[1]):
        base = 2 * ids[:, k : k + 1]
        hit = (lane == base) | (lane == base + 1)
        hit = hit | (lane == base + LANES // 2) | (lane == base + LANES // 2 + 1)
        value = jnp.sum(jnp.where(hit, marks, 0.0), axis=1, keepdims=True)
        routes = jnp.where(lane == k, value, routes)
    rg_ref[...] = routes[:, 0 : ids.shape[1]]

    def drain(s, carry):
        x_copy(s).wait_send()
        y_copy(s).wait_send()
        xh_copy(s).wait_send()
        yh_copy(s).wait_send()
        for which in range(4):
            core_copy(s, which).wait_send()
        swap_copy(s).wait_send()
        for to in range(2):
            fa_copy(s, to).wait_send()
            fb_copy(s, to).wait_send()
        ta_copy(s).wait_send()
        tb_copy(s).wait_send()

        @pl.when(s > 0)
        def _():
            z_copy(s).wait_send()
            zo_copy(s).wait_send()

        return carry

    lax.fori_loop(0, planes, drain, 0)


def kernel_body(tokens, expert_ids, route_weight, out_grad, gate_weight, up_weight, down_weight):
    dp_size, ex_size = lax.axis_size("dp"), lax.axis_size("expert")
    planes, experts = dp_size // 2, dp_size * ex_size // 2
    tok_count, width = tokens.shape
    half = gate_weight.shape[2]
    tile = TILE
    full = 2 * width + LANES
    bf16, f32 = jnp.bfloat16, jnp.float32
    every = planes * 8 * tok_count
    dma = pltpu.SemaphoreType.DMA
    vmem = pl.BlockSpec(memory_space=pltpu.VMEM)
    hbm = pl.BlockSpec(memory_space=pl.ANY)
    shape = jax.ShapeDtypeStruct
    sems = [dma((3,)), dma((planes - 1,)), dma((planes - 1,))]
    sems += [dma((planes,)) for _ in range(8)]
    sems += [dma((planes, 4))] * 2 + [dma((planes,))] * 2 + [dma((planes, 2))] * 4
    sems += [dma((planes,))] * 4 + [dma((planes - 1,))] * 2
    return pl.pallas_call(
        functools.partial(expert_kernel, planes, tok_count, width, half, experts, tile),
        out_shape=(
            shape(tokens.shape, bf16),
            shape(tokens.shape, bf16),
            shape(route_weight.shape, f32),
            shape(gate_weight.shape, bf16),
            shape(up_weight.shape, bf16),
            shape(down_weight.shape, bf16),
        ),
        in_specs=[vmem] * 4 + [hbm] * 3,
        out_specs=[vmem] * 6,
        scratch_shapes=[
            pltpu.VMEM((planes, 2, 4, tok_count, full), bf16),
            pltpu.VMEM((planes, 2, 4, tok_count, full), bf16),
            pltpu.VMEM((planes, 4, tok_count, full), bf16),
            pltpu.VMEM((planes, 4, tok_count, full), bf16),
            pltpu.VMEM((planes, 2, tok_count, width), bf16),
            pltpu.VMEM((planes, 2, tok_count, width + LANES), bf16),
            pltpu.VMEM((planes, tok_count, width), bf16),
            pltpu.VMEM((planes, tok_count, width + LANES), bf16),
            pltpu.VMEM((planes, tok_count, width), bf16),
            pltpu.VMEM((planes, tok_count, width + LANES), bf16),
            pltpu.VMEM((planes - 1, tok_count, full), bf16),
            pltpu.VMEM((planes - 1, tok_count, full), bf16),
            pltpu.VMEM((tok_count, full), f32),
            pltpu.VMEM((every, half), bf16),
            pltpu.VMEM((every, 2 * half), bf16),
            pltpu.VMEM(gate_weight.shape[1:], bf16),
            pltpu.VMEM(up_weight.shape[1:], bf16),
            pltpu.VMEM(down_weight.shape[1:], bf16),
        ] + sems,
        compiler_params=pltpu.CompilerParams(
            collective_id=0, has_side_effects=True, vmem_limit_bytes=60 * 1024 * 1024
        ),
    )(tokens, expert_ids, route_weight, out_grad, gate_weight, up_weight, down_weight)


def solution(mesh):
    in_specs = (
        P(("dp", "expert"), None),
        P(("dp", "expert"), None),
        P(("dp", "expert"), None),
        P(("dp", "expert"), None),
        P(("dp", "expert"), None, None),
        P(("dp", "expert"), None, None),
        P(("dp", "expert"), None, None),
    )
    out_specs = (
        P(("dp", "expert"), None),
        P(("dp", "expert"), None),
        P(("dp", "expert"), None),
        P(("dp", "expert"), None, None),
        P(("dp", "expert"), None, None),
        P(("dp", "expert"), None, None),
    )
    dp_size, ex_size = mesh.shape["dp"], mesh.shape["expert"]
    pieces = dp_size * ex_size

    def step(tokens, expert_ids, *rest):
        capacity = 2 * (tokens.shape[0] * expert_ids.shape[1] // (pieces // 2))
        fits = ex_size == 4 and dp_size >= 4 and dp_size % 2 == 0 and 3 * pieces // 2 <= LANES
        fits = fits and pieces <= LANES // 2 and tokens.shape[1] % (2 * TILE) == 0
        form = kernel_body if fits and capacity >= tokens.shape[0] else body
        return form(tokens, expert_ids, *rest)

    return jax.shard_map(step, mesh=mesh, in_specs=in_specs, out_specs=out_specs, check_vma=False)
```

```python
import functools

import jax
import jax.numpy as jnp
from jax import lax
from jax.experimental import pallas as pl
from jax.experimental.pallas import tpu as pltpu
from jax.sharding import PartitionSpec as P

LANES = 128
TILE = 256
PARTS = 4


def from_partner(shard, axis, apart):
    return lax.ppermute(shard, axis, [(i, i ^ 1 << apart) for i in range(lax.axis_size(axis))])


def contract(left_op, right_op, left_dim, right_dim):
    return lax.dot_general(
        left_op,
        right_op,
        (((left_dim,), (right_dim,)), ((), ())),
        preferred_element_type=jnp.float32,
    )


def deliver(buffer, dp_size, ex_size, experts, capacity, backward):
    feat_width = buffer.shape[1]
    doubled = jnp.broadcast_to(
        buffer.reshape(experts, 1, capacity, feat_width), (experts, 2, capacity, feat_width)
    )
    doubled = doubled.reshape(dp_size, ex_size, capacity, feat_width)
    if backward:
        arrived = lax.all_to_all(
            lax.all_to_all(doubled, "dp", split_axis=0, concat_axis=0, tiled=True),
            "expert",
            split_axis=1,
            concat_axis=1,
            tiled=True,
        )
    else:
        arrived = lax.all_to_all(
            lax.all_to_all(doubled, "dp", split_axis=0, concat_axis=0, tiled=True),
            "expert",
            split_axis=1,
            concat_axis=1,
            tiled=True,
        )
    return arrived.reshape(-1, feat_width)


def bring_back(partials_in, dp_size, ex_size, experts, capacity, half_index, backward):
    feat_width = partials_in.shape[1]
    if backward:
        partner = from_partner(partials_in, "expert", 0)
    else:
        partner = from_partner(partials_in, "expert", 0)
    summed = (partials_in.astype(jnp.float32) + partner.astype(jnp.float32)).astype(jnp.bfloat16)
    summed = summed.reshape(dp_size, ex_size, capacity, feat_width)
    own_half = lax.dynamic_slice_in_dim(summed, half_index * (capacity // 2), capacity // 2, 2)
    if backward:
        returned = lax.all_to_all(
            lax.all_to_all(own_half, "dp", split_axis=0, concat_axis=0, tiled=True),
            "expert",
            split_axis=1,
            concat_axis=1,
            tiled=True,
        )
    else:
        returned = lax.all_to_all(
            lax.all_to_all(own_half, "dp", split_axis=0, concat_axis=0, tiled=True),
            "expert",
            split_axis=1,
            concat_axis=1,
            tiled=True,
        )
    merged = returned.reshape(experts, capacity, feat_width)
    return merged.reshape(experts * capacity, feat_width)


def body(tokens, expert_ids, route_weight, out_grad, gate_weight, up_weight, down_weight):
    dp_size = lax.axis_size("dp")
    ex_size = lax.axis_size("expert")
    tok_count, feat_width = tokens.shape
    top_count = expert_ids.shape[1]
    experts = dp_size * ex_size // 2
    assigned = tok_count * top_count
    capacity = 2 * (assigned // experts)
    half_index = lax.axis_index("expert") % 2
    flat_ids = expert_ids.reshape(-1)
    onehot = (flat_ids[:, None] == jnp.arange(experts, dtype=jnp.int32)[None, :]).astype(jnp.int32)
    before = jnp.cumsum(onehot, axis=0) - onehot
    slot_ids = jnp.sum(before * onehot, axis=1)
    place_row = flat_ids * capacity + slot_ids
    source = (
        jnp.full((experts * capacity,), -1, jnp.int32)
        .at[place_row]
        .set(jnp.arange(assigned, dtype=jnp.int32))
    )
    filled = source >= 0
    assign = jnp.maximum(source, 0)
    rows_tok = assign // top_count
    send_rows = jnp.where(filled[:, None], tokens[rows_tok], jnp.zeros((), jnp.bfloat16))
    in_rows = deliver(send_rows, dp_size, ex_size, experts, capacity, False)
    w_gate = gate_weight[0]
    w_up = up_weight[0]
    w_down = down_weight[0]
    gate_act = jnp.dot(in_rows, w_gate, preferred_element_type=jnp.float32)
    up_act = jnp.dot(in_rows, w_up, preferred_element_type=jnp.float32)
    sig_gate = jax.nn.sigmoid(gate_act)
    hidden = (gate_act * sig_gate * up_act).astype(jnp.bfloat16)
    partial_value = jnp.dot(hidden, w_down, preferred_element_type=jnp.float32).astype(jnp.bfloat16)
    expert_table = bring_back(partial_value, dp_size, ex_size, experts, capacity, half_index, False)
    expert_rows = expert_table[place_row].reshape(tok_count, top_count, feat_width)
    layer_out = jnp.sum(route_weight[:, :, None] * expert_rows.astype(jnp.float32), axis=1).astype(
        jnp.bfloat16
    )
    route_grad = jnp.einsum("tkd,td->tk", expert_rows, out_grad, preferred_element_type=jnp.float32)
    scaled = (route_weight[:, :, None] * out_grad[:, None, :].astype(jnp.float32)).astype(
        jnp.bfloat16
    )
    scaled = scaled.reshape(assigned, feat_width)
    send_grad = jnp.where(filled[:, None], scaled[assign], jnp.zeros((), jnp.bfloat16))
    grad_rows = deliver(send_grad, dp_size, ex_size, experts, capacity, True)
    hidden_grad = contract(grad_rows, w_down, 1, 1)
    gate_pre = (hidden_grad * up_act * sig_gate * (1.0 + gate_act * (1.0 - sig_gate))).astype(
        jnp.bfloat16
    )
    up_pre = (hidden_grad * gate_act * sig_gate).astype(jnp.bfloat16)
    partial_grad = (contract(gate_pre, w_gate, 1, 1) + contract(up_pre, w_up, 1, 1)).astype(
        jnp.bfloat16
    )
    gate_grad = contract(in_rows, gate_pre, 0, 0).astype(jnp.bfloat16)
    up_grad = contract(in_rows, up_pre, 0, 0).astype(jnp.bfloat16)
    down_grad = contract(hidden, grad_rows, 0, 0).astype(jnp.bfloat16)
    grad_table = bring_back(partial_grad, dp_size, ex_size, experts, capacity, half_index, True)
    expert_grad = grad_table[place_row].reshape(tok_count, top_count, feat_width)
    token_grad = jnp.sum(expert_grad.astype(jnp.float32), axis=1).astype(jnp.bfloat16)
    return (layer_out, token_grad, route_grad, gate_grad[None], up_grad[None], down_grad[None])


def expert_kernel(
    planes, tok_count, width, half, experts, tile,
    tok_ref, ids_ref, rw_ref, og_ref, wg_hbm, wu_hbm, wd_hbm,
    lo_ref, tg_ref, rg_ref, gg_ref, ug_ref, dg_ref,
    rows, parts, swapped, summed, first_a, first_b, turn_a, turn_b, second_a, second_b,
    zsend, zrecv, zown, hidden_all, pre_all, wg_ref, wu_ref, wd_ref,
    gg_buf, ug_buf, dg_buf, grad_sem, load_sem, z_ss, z_rs, x_ss, x_rs, y_ss, y_rs, xh_ss, xh_rs, yh_ss, yh_rs,
    core_ss, core_rs, swap_ss, swap_rs, fa_ss, fa_rs, fb_ss, fb_rs,
    ta_ss, ta_rs, tb_ss, tb_rs, zo_ss, zo_rs,
):
    f32, bf16 = jnp.float32, jnp.bfloat16
    dp, ex = lax.axis_index("dp"), lax.axis_index("expert")
    z, y, x, c = dp // 2, dp % 2, ex // 2, ex % 2
    piece = dp * lax.axis_size("expert") + ex
    mine = piece // 2
    full = 2 * width + LANES
    x_dev, y_dev, core_dev = (dp, (1 - x) * 2 + c), (z * 2 + 1 - y, ex), (dp, x * 2 + 1 - c)
    here, over_x, over_y, over_xy = y * 2 + x, y * 2 + 1 - x, (1 - y) * 2 + x, (1 - y) * 2 + 1 - x
    left, right = pl.ds(0, width), pl.ds(width, width + LANES)

    def remote(src, dst, send, recv, device):
        return pltpu.make_async_remote_copy(
            src_ref=src, dst_ref=dst, send_sem=send, recv_sem=recv,
            device_id=device, device_id_type=pl.DeviceIdType.MESH,
        )

    def landed(dst, send, recv):
        remote(dst, dst, send, recv, core_dev).wait_recv()

    def plane(step):
        return (z + planes - step) % planes

    def load(i):
        src = (wg_hbm, wu_hbm, wd_hbm)[i]
        dst = (wg_ref, wu_ref, wd_ref)[i]
        return pltpu.make_async_copy(src.at[0], dst, load_sem.at[i])

    for i in range(3):
        load(i).start()

    lane = lax.broadcasted_iota(jnp.int32, (tok_count, LANES), 1)
    ids, weights = ids_ref[...].T, rw_ref[...].T
    table = [jnp.zeros((tok_count, LANES), f32) for _ in range(3)]
    for k in range(ids.shape[1]):
        for part in range(3):
            hit = lane == ids[:, k : k + 1] + part * experts
            table[part] = jnp.where(hit, weights[:, k : k + 1], table[part])
    head = table[0].astype(bf16).astype(f32)
    mid = table[1] - table[1].astype(bf16).astype(f32)
    mid = mid.astype(bf16).astype(f32)
    rest = table[2] - table[2].astype(bf16).astype(f32)
    rest = rest - rest.astype(bf16).astype(f32)
    rows[z, c, here, :, pl.ds(0, width)] = tok_ref[...]
    rows[z, c, here, :, pl.ds(width, width)] = og_ref[...]
    rows[z, c, here, :, pl.ds(2 * width, LANES)] = (head + mid + rest).astype(bf16)

    barrier = pltpu.get_barrier_semaphore()
    peers = [x_dev, y_dev, core_dev]
    peers += [(((z + d) % planes) * 2 + y, ex) for d in range(1, planes)]
    for peer in peers:
        pl.semaphore_signal(barrier, inc=1, device_id=peer, device_id_type=pl.DeviceIdType.MESH)
    pl.semaphore_wait(barrier, len(peers))

    def z_copy(d):
        slot = rows.at[z, c, here]
        peer = (((z + d) % planes) * 2 + y, ex)
        return remote(slot, slot, z_ss.at[d - 1], z_rs.at[d - 1], peer)

    def x_copy(s):
        slot = rows.at[plane(s), c, here]
        return remote(slot, slot, x_ss.at[s], x_rs.at[s], x_dev)

    def y_copy(s):
        slot = rows.at[plane(s), c, here]
        return remote(slot, slot, y_ss.at[s], y_rs.at[s], y_dev)

    def xh_copy(s):
        slot = rows.at[plane(s), c, over_y, :, left]
        return remote(slot, slot, xh_ss.at[s], xh_rs.at[s], x_dev)

    def yh_copy(s):
        slot = rows.at[plane(s), c, over_x, :, right]
        return remote(slot, slot, yh_ss.at[s], yh_rs.at[s], y_dev)

    def core_copy(s, which):
        slot = rows.at[plane(s), c, (here, over_x, over_y, over_xy)[which]]
        return remote(slot, slot, core_ss.at[s, which], core_rs.at[s, which], core_dev)

    def swap_copy(s):
        q = plane(s)
        return remote(parts.at[q, 1 - c], swapped.at[q], swap_ss.at[s], swap_rs.at[s], core_dev)

    def fa_copy(s, to_y):
        src = summed.at[plane(s), to_y * 2 + 1 - x, :, left]
        return remote(src, first_a.at[s, to_y], fa_ss.at[s, to_y], fa_rs.at[s, to_y], x_dev)

    def fb_copy(s, to_x):
        src = summed.at[plane(s), (1 - y) * 2 + to_x, :, right]
        return remote(src, first_b.at[s, to_x], fb_ss.at[s, to_x], fb_rs.at[s, to_x], y_dev)

    def ta_copy(s):
        return remote(turn_a.at[s], second_a.at[s], ta_ss.at[s], ta_rs.at[s], y_dev)

    def tb_copy(s):
        return remote(turn_b.at[s], second_b.at[s], tb_ss.at[s], tb_rs.at[s], x_dev)

    def zo_copy(s):
        peer = (plane(s) * 2 + y, ex)
        return remote(zsend.at[s - 1], zrecv.at[s - 1], zo_ss.at[s - 1], zo_rs.at[s - 1], peer)

    def gather_one(s):
        @pl.when(s > 0)
        def _():
            landed(rows.at[plane(s), c, here], z_ss.at[s - 1], z_rs.at[s - 1])

        x_copy(s).start()
        y_copy(s).start()
        core_copy(s, 0).start()

    def gather_two(s):
        q = plane(s)
        landed(rows.at[q, c, over_x], x_ss.at[s], x_rs.at[s])
        yh_copy(s).start()
        core_copy(s, 1).start()
        landed(rows.at[q, c, over_y], y_ss.at[s], y_rs.at[s])
        xh_copy(s).start()
        core_copy(s, 2).start()

    def gather_three(s):
        q = plane(s)
        landed(rows.at[q, c, over_xy, :, left], xh_ss.at[s], xh_rs.at[s])
        landed(rows.at[q, c, over_xy, :, right], yh_ss.at[s], yh_rs.at[s])
        core_copy(s, 3).start()

    group = 8 * tok_count
    glane = lax.broadcasted_iota(jnp.int32, (group, LANES), 1)

    def compute(s):
        q = plane(s)
        for which, slot in enumerate((here, over_x, over_y, over_xy)):
            landed(rows.at[q, 1 - c, slot], core_ss.at[s, which], core_rs.at[s, which])
        x_in = rows[q, :, :, :, 0:width].reshape(group, width)
        g_in = rows[q, :, :, :, width : 2 * width].reshape(group, width)
        gate = contract(x_in, wg_ref[...], 1, 0)
        up = contract(x_in, wu_ref[...], 1, 0)
        back = contract(g_in, wd_ref[...], 1, 1)
        tab = rows[q, :, :, :, 2 * width : full].reshape(group, LANES).astype(f32)
        own = (glane == mine) | (glane == mine + experts) | (glane == mine + 2 * experts)
        weight = jnp.sum(jnp.where(own, tab, 0.0), axis=1, keepdims=True)
        sig = 1.0 / (1.0 + jnp.exp(-gate))
        act = gate * sig
        hidden = act * up
        route = jnp.sum(hidden * back, axis=1, keepdims=True)
        coarse = route.astype(bf16).astype(f32)
        fine = route - coarse
        marks = jnp.where(glane == piece, coarse, jnp.where(glane == piece + LANES // 2, fine, 0.0))
        back = weight * back
        hid = (weight * hidden).astype(bf16)
        gate_pre = (back * up * sig * (1.0 + gate * (1.0 - sig))).astype(bf16)
        up_pre = (back * act).astype(bf16)
        at = pl.ds(pl.multiple_of(q * group, group), group)
        hidden_all[at, :] = hid
        pre_all[at, 0:half] = gate_pre
        pre_all[at, half : 2 * half] = up_pre
        shape = (2, 4, tok_count)
        for n in range(0, width, 2 * tile):
            cols = slice(n, n + 2 * tile)
            out = contract(hid, wd_ref[:, cols], 1, 0)
            parts[q, :, :, :, cols] = out.astype(bf16).reshape(shape + (2 * tile,))
            grad = contract(gate_pre, wg_ref[cols, :], 1, 1) + contract(up_pre, wu_ref[cols, :], 1, 1)
            after = slice(width + n, width + n + 2 * tile)
            parts[q, :, :, :, after] = grad.astype(bf16).reshape(shape + (2 * tile,))
        parts[q, :, :, :, 2 * width : full] = marks.astype(bf16).reshape(shape + (LANES,))
        swap_copy(s).start()

    def reduce_one(s):
        q = plane(s)
        landed(swapped.at[q], swap_ss.at[s], swap_rs.at[s])

        def add(t, carry):
            total = parts[q, c, t].astype(f32) + swapped[q, t].astype(f32)
            summed[q, t] = total.astype(bf16)
            return carry

        lax.fori_loop(0, 4, add, 0)
        fa_copy(s, 1 - y).start()
        fb_copy(s, 1 - x).start()
        fa_copy(s, y).start()
        fb_copy(s, x).start()

    def reduce_two(s):
        q = plane(s)
        landed(first_a.at[s, 1 - y], fa_ss.at[s, 1 - y], fa_rs.at[s, 1 - y])
        total = summed[q, over_y, :, 0:width].astype(f32) + first_a[s, 1 - y].astype(f32)
        turn_a[s] = total.astype(bf16)
        ta_copy(s).start()
        landed(first_b.at[s, 1 - x], fb_ss.at[s, 1 - x], fb_rs.at[s, 1 - x])
        total = summed[q, over_x, :, width:full].astype(f32) + first_b[s, 1 - x].astype(f32)
        turn_b[s] = total.astype(bf16)
        tb_copy(s).start()

    def reduce_three(s):
        q = plane(s)
        landed(first_a.at[s, y], fa_ss.at[s, y], fa_rs.at[s, y])
        landed(first_b.at[s, x], fb_ss.at[s, x], fb_rs.at[s, x])
        landed(second_a.at[s], ta_ss.at[s], ta_rs.at[s])
        landed(second_b.at[s], tb_ss.at[s], tb_rs.at[s])
        total_a = summed[q, here, :, 0:width].astype(f32) + first_a[s, y].astype(f32)
        total_a = total_a + second_a[s].astype(f32)
        total_b = summed[q, here, :, width:full].astype(f32) + first_b[s, x].astype(f32)
        total_b = total_b + second_b[s].astype(f32)

        @pl.when(s == 0)
        def _():
            zown[:, 0:width] = total_a
            zown[:, width:full] = total_b

        @pl.when(s > 0)
        def _():
            zsend[s - 1, :, 0:width] = total_a.astype(bf16)
            zsend[s - 1, :, width:full] = total_b.astype(bf16)
            zo_copy(s).start()

    every = planes * group
    tiles = width // tile

    def grad_copy(t, i):
        cols = pl.ds(pl.multiple_of(t * tile, tile), tile)
        src = (gg_buf.at[cols, :], ug_buf.at[cols, :], dg_buf.at[:, cols])[i]
        dst = (gg_ref.at[0, cols, :], ug_ref.at[0, cols, :], dg_ref.at[0, :, cols])[i]
        return pltpu.make_async_copy(src, dst, grad_sem.at[t, i])

    def weight_grads(t, carry):
        cols = pl.ds(pl.multiple_of(t * tile, tile), tile)
        x_in = rows[:, :, :, :, cols].reshape(every, tile)
        after = pl.ds(pl.multiple_of(width + t * tile, tile), tile)
        g_in = rows[:, :, :, :, after].reshape(every, tile)
        both = contract(x_in, pre_all[...], 0, 0).astype(bf16)
        gg_buf[cols, :] = both[:, 0:half]
        ug_buf[cols, :] = both[:, half : 2 * half]
        dg_buf[:, cols] = contract(hidden_all[...], g_in, 0, 0).astype(bf16)
        for i in range(3):
            grad_copy(t, i).start()
        return carry

    for d in range(1, planes):
        z_copy(d).start()

    def step(i, carry):
        def stage(at, run):
            @pl.when((i >= at) & (i < at + planes))
            def _():
                run(i - at)

        stage(0, gather_one)
        stage(1, gather_two)
        stage(2, gather_three)

        @pl.when(i == 3)
        def _():
            for j in range(3):
                load(j).wait()

        stage(3, compute)
        stage(4, reduce_one)
        stage(5, reduce_two)
        stage(6, reduce_three)

        @pl.when(i >= planes + 3)
        def _():
            j = i - (planes + 3)
            lax.fori_loop((j * tiles) // 3, ((j + 1) * tiles) // 3, weight_grads, 0)

        return carry

    lax.fori_loop(0, planes + 6, step, 0)

    total = zown[...]
    for s in range(1, planes):
        landed(zrecv.at[s - 1], zo_ss.at[s - 1], zo_rs.at[s - 1])
        total = total + zrecv[s - 1].astype(f32)
    lo_ref[...] = total[:, 0:width].astype(bf16)
    tg_ref[...] = total[:, width : 2 * width].astype(bf16)
    marks = total[:, 2 * width : full]
    routes = jnp.zeros((tok_count, LANES), f32)
    for k in range(ids.shape[1]):
        base = 2 * ids[:, k : k + 1]
        hit = (lane == base) | (lane == base + 1)
        hit = hit | (lane == base + LANES // 2) | (lane == base + LANES // 2 + 1)
        value = jnp.sum(jnp.where(hit, marks, 0.0), axis=1, keepdims=True)
        routes = jnp.where(lane == k, value, routes)
    rg_ref[...] = routes.T[0 : ids.shape[1], :]

    def drain(s, carry):
        x_copy(s).wait_send()
        y_copy(s).wait_send()
        xh_copy(s).wait_send()
        yh_copy(s).wait_send()
        for which in range(4):
            core_copy(s, which).wait_send()
        swap_copy(s).wait_send()
        for to in range(2):
            fa_copy(s, to).wait_send()
            fb_copy(s, to).wait_send()
        ta_copy(s).wait_send()
        tb_copy(s).wait_send()

        @pl.when(s > 0)
        def _():
            z_copy(s).wait_send()
            zo_copy(s).wait_send()

        return carry

    lax.fori_loop(0, planes, drain, 0)

    def stored(t, carry):
        for i in range(3):
            grad_copy(t, i).wait()
        return carry

    lax.fori_loop(0, tiles, stored, 0)


def finish_kernel(
    lo_in, tg_in, rg_in, gg_in, ug_in, dg_in, lo_ref, tg_ref, rg_ref, gg_ref, ug_ref, dg_ref,
    gg_buf, ug_buf, dg_buf, in_sem, out_sem,
):
    trips = ((gg_in, gg_buf, gg_ref), (ug_in, ug_buf, ug_ref), (dg_in, dg_buf, dg_ref))

    def pair(i, j):
        src, buf, dst = trips[i]
        count = buf.shape[0] // PARTS
        at = pl.ds(j * count, count)
        into = pltpu.make_async_copy(src.at[0, at, :], buf.at[at, :], in_sem.at[i, j])
        return into, pltpu.make_async_copy(buf.at[at, :], dst.at[0, at, :], out_sem.at[i, j])

    order = [(i, j) for i in range(3) for j in range(PARTS)]
    for i, j in order:
        pair(i, j)[0].start()
    lo_ref[...] = lo_in[...]
    tg_ref[...] = tg_in[...]
    rg_ref[...] = rg_in[...]
    for i, j in order:
        pair(i, j)[0].wait()
        pair(i, j)[1].start()
    for i, j in order:
        pair(i, j)[1].wait()


def kernel_body(tokens, expert_ids, route_weight, out_grad, gate_weight, up_weight, down_weight):
    dp_size, ex_size = lax.axis_size("dp"), lax.axis_size("expert")
    planes, experts = dp_size // 2, dp_size * ex_size // 2
    tok_count, width = tokens.shape
    half = gate_weight.shape[2]
    tile = TILE
    full = 2 * width + LANES
    bf16, f32 = jnp.bfloat16, jnp.float32
    every = planes * 8 * tok_count
    dma = pltpu.SemaphoreType.DMA
    vmem = pl.BlockSpec(memory_space=pltpu.VMEM)
    hbm = pl.BlockSpec(memory_space=pl.ANY)
    shape = jax.ShapeDtypeStruct
    sems = [dma((width // tile, 3)), dma((3,)), dma((planes - 1,)), dma((planes - 1,))]
    sems += [dma((planes,)) for _ in range(8)]
    sems += [dma((planes, 4))] * 2 + [dma((planes,))] * 2 + [dma((planes, 2))] * 4
    sems += [dma((planes,))] * 4 + [dma((planes - 1,))] * 2
    outs = pl.pallas_call(
        functools.partial(expert_kernel, planes, tok_count, width, half, experts, tile),
        out_shape=(
            shape(tokens.shape, bf16),
            shape(tokens.shape, bf16),
            shape(route_weight.shape[::-1], f32),
            shape(gate_weight.shape, bf16),
            shape(up_weight.shape, bf16),
            shape(down_weight.shape, bf16),
        ),
        in_specs=[vmem] * 4 + [hbm] * 3,
        out_specs=[vmem] * 3 + [hbm] * 3,
        scratch_shapes=[
            pltpu.VMEM((planes, 2, 4, tok_count, full), bf16),
            pltpu.VMEM((planes, 2, 4, tok_count, full), bf16),
            pltpu.VMEM((planes, 4, tok_count, full), bf16),
            pltpu.VMEM((planes, 4, tok_count, full), bf16),
            pltpu.VMEM((planes, 2, tok_count, width), bf16),
            pltpu.VMEM((planes, 2, tok_count, width + LANES), bf16),
            pltpu.VMEM((planes, tok_count, width), bf16),
            pltpu.VMEM((planes, tok_count, width + LANES), bf16),
            pltpu.VMEM((planes, tok_count, width), bf16),
            pltpu.VMEM((planes, tok_count, width + LANES), bf16),
            pltpu.VMEM((planes - 1, tok_count, full), bf16),
            pltpu.VMEM((planes - 1, tok_count, full), bf16),
            pltpu.VMEM((tok_count, full), f32),
            pltpu.VMEM((every, half), bf16),
            pltpu.VMEM((every, 2 * half), bf16),
            pltpu.VMEM(gate_weight.shape[1:], bf16),
            pltpu.VMEM(up_weight.shape[1:], bf16),
            pltpu.VMEM(down_weight.shape[1:], bf16),
            pltpu.VMEM(gate_weight.shape[1:], bf16),
            pltpu.VMEM(up_weight.shape[1:], bf16),
            pltpu.VMEM(down_weight.shape[1:], bf16),
        ] + sems,
        compiler_params=pltpu.CompilerParams(
            collective_id=0, has_side_effects=True, vmem_limit_bytes=60 * 1024 * 1024
        ),
    )(tokens, expert_ids.T, route_weight.T, out_grad, gate_weight, up_weight, down_weight)
    lo, tg, rg, gg, ug, dg = pl.pallas_call(
        finish_kernel,
        out_shape=tuple(shape(o.shape, o.dtype) for o in outs),
        in_specs=[vmem] * 3 + [hbm] * 3,
        out_specs=[vmem] * 3 + [hbm] * 3,
        scratch_shapes=[
            pltpu.VMEM(gate_weight.shape[1:], bf16),
            pltpu.VMEM(up_weight.shape[1:], bf16),
            pltpu.VMEM(down_weight.shape[1:], bf16),
            dma((3, PARTS)),
            dma((3, PARTS)),
        ],
        compiler_params=pltpu.CompilerParams(vmem_limit_bytes=60 * 1024 * 1024),
    )(*outs)
    return lo, tg, rg.T, gg, ug, dg


def solution(mesh):
    in_specs = (
        P(("dp", "expert"), None),
        P(("dp", "expert"), None),
        P(("dp", "expert"), None),
        P(("dp", "expert"), None),
        P(("dp", "expert"), None, None),
        P(("dp", "expert"), None, None),
        P(("dp", "expert"), None, None),
    )
    out_specs = (
        P(("dp", "expert"), None),
        P(("dp", "expert"), None),
        P(("dp", "expert"), None),
        P(("dp", "expert"), None, None),
        P(("dp", "expert"), None, None),
        P(("dp", "expert"), None, None),
    )
    dp_size, ex_size = mesh.shape["dp"], mesh.shape["expert"]
    pieces = dp_size * ex_size

    def step(tokens, expert_ids, *rest):
        capacity = 2 * (tokens.shape[0] * expert_ids.shape[1] // (pieces // 2))
        fits = ex_size == 4 and dp_size >= 4 and dp_size % 2 == 0 and 3 * pieces // 2 <= LANES
        fits = fits and pieces <= LANES // 2 and tokens.shape[1] % (2 * TILE) == 0
        form = kernel_body if fits and capacity >= tokens.shape[0] else body
        return form(tokens, expert_ids, *rest)

    return jax.shard_map(step, mesh=mesh, in_specs=in_specs, out_specs=out_specs, check_vma=False)
```

```python
import functools

import jax
import jax.numpy as jnp
from jax import lax
from jax.experimental import pallas as pl
from jax.experimental.pallas import tpu as pltpu
from jax.sharding import PartitionSpec as P

LANES = 128
TILE = 256
PARTS = 4


def from_partner(shard, axis, apart):
    return lax.ppermute(shard, axis, [(i, i ^ 1 << apart) for i in range(lax.axis_size(axis))])


def contract(left_op, right_op, left_dim, right_dim):
    return lax.dot_general(
        left_op,
        right_op,
        (((left_dim,), (right_dim,)), ((), ())),
        preferred_element_type=jnp.float32,
    )


def deliver(buffer, dp_size, ex_size, experts, capacity, backward):
    feat_width = buffer.shape[1]
    doubled = jnp.broadcast_to(
        buffer.reshape(experts, 1, capacity, feat_width), (experts, 2, capacity, feat_width)
    )
    doubled = doubled.reshape(dp_size, ex_size, capacity, feat_width)
    if backward:
        arrived = lax.all_to_all(
            lax.all_to_all(doubled, "dp", split_axis=0, concat_axis=0, tiled=True),
            "expert",
            split_axis=1,
            concat_axis=1,
            tiled=True,
        )
    else:
        arrived = lax.all_to_all(
            lax.all_to_all(doubled, "dp", split_axis=0, concat_axis=0, tiled=True),
            "expert",
            split_axis=1,
            concat_axis=1,
            tiled=True,
        )
    return arrived.reshape(-1, feat_width)


def bring_back(partials_in, dp_size, ex_size, experts, capacity, half_index, backward):
    feat_width = partials_in.shape[1]
    if backward:
        partner = from_partner(partials_in, "expert", 0)
    else:
        partner = from_partner(partials_in, "expert", 0)
    summed = (partials_in.astype(jnp.float32) + partner.astype(jnp.float32)).astype(jnp.bfloat16)
    summed = summed.reshape(dp_size, ex_size, capacity, feat_width)
    own_half = lax.dynamic_slice_in_dim(summed, half_index * (capacity // 2), capacity // 2, 2)
    if backward:
        returned = lax.all_to_all(
            lax.all_to_all(own_half, "dp", split_axis=0, concat_axis=0, tiled=True),
            "expert",
            split_axis=1,
            concat_axis=1,
            tiled=True,
        )
    else:
        returned = lax.all_to_all(
            lax.all_to_all(own_half, "dp", split_axis=0, concat_axis=0, tiled=True),
            "expert",
            split_axis=1,
            concat_axis=1,
            tiled=True,
        )
    merged = returned.reshape(experts, capacity, feat_width)
    return merged.reshape(experts * capacity, feat_width)


def body(tokens, expert_ids, route_weight, out_grad, gate_weight, up_weight, down_weight):
    dp_size = lax.axis_size("dp")
    ex_size = lax.axis_size("expert")
    tok_count, feat_width = tokens.shape
    top_count = expert_ids.shape[1]
    experts = dp_size * ex_size // 2
    assigned = tok_count * top_count
    capacity = 2 * (assigned // experts)
    half_index = lax.axis_index("expert") % 2
    flat_ids = expert_ids.reshape(-1)
    onehot = (flat_ids[:, None] == jnp.arange(experts, dtype=jnp.int32)[None, :]).astype(jnp.int32)
    before = jnp.cumsum(onehot, axis=0) - onehot
    slot_ids = jnp.sum(before * onehot, axis=1)
    place_row = flat_ids * capacity + slot_ids
    source = (
        jnp.full((experts * capacity,), -1, jnp.int32)
        .at[place_row]
        .set(jnp.arange(assigned, dtype=jnp.int32))
    )
    filled = source >= 0
    assign = jnp.maximum(source, 0)
    rows_tok = assign // top_count
    send_rows = jnp.where(filled[:, None], tokens[rows_tok], jnp.zeros((), jnp.bfloat16))
    in_rows = deliver(send_rows, dp_size, ex_size, experts, capacity, False)
    w_gate = gate_weight[0]
    w_up = up_weight[0]
    w_down = down_weight[0]
    gate_act = jnp.dot(in_rows, w_gate, preferred_element_type=jnp.float32)
    up_act = jnp.dot(in_rows, w_up, preferred_element_type=jnp.float32)
    sig_gate = jax.nn.sigmoid(gate_act)
    hidden = (gate_act * sig_gate * up_act).astype(jnp.bfloat16)
    partial_value = jnp.dot(hidden, w_down, preferred_element_type=jnp.float32).astype(jnp.bfloat16)
    expert_table = bring_back(partial_value, dp_size, ex_size, experts, capacity, half_index, False)
    expert_rows = expert_table[place_row].reshape(tok_count, top_count, feat_width)
    layer_out = jnp.sum(route_weight[:, :, None] * expert_rows.astype(jnp.float32), axis=1).astype(
        jnp.bfloat16
    )
    route_grad = jnp.einsum("tkd,td->tk", expert_rows, out_grad, preferred_element_type=jnp.float32)
    scaled = (route_weight[:, :, None] * out_grad[:, None, :].astype(jnp.float32)).astype(
        jnp.bfloat16
    )
    scaled = scaled.reshape(assigned, feat_width)
    send_grad = jnp.where(filled[:, None], scaled[assign], jnp.zeros((), jnp.bfloat16))
    grad_rows = deliver(send_grad, dp_size, ex_size, experts, capacity, True)
    hidden_grad = contract(grad_rows, w_down, 1, 1)
    gate_pre = (hidden_grad * up_act * sig_gate * (1.0 + gate_act * (1.0 - sig_gate))).astype(
        jnp.bfloat16
    )
    up_pre = (hidden_grad * gate_act * sig_gate).astype(jnp.bfloat16)
    partial_grad = (contract(gate_pre, w_gate, 1, 1) + contract(up_pre, w_up, 1, 1)).astype(
        jnp.bfloat16
    )
    gate_grad = contract(in_rows, gate_pre, 0, 0).astype(jnp.bfloat16)
    up_grad = contract(in_rows, up_pre, 0, 0).astype(jnp.bfloat16)
    down_grad = contract(hidden, grad_rows, 0, 0).astype(jnp.bfloat16)
    grad_table = bring_back(partial_grad, dp_size, ex_size, experts, capacity, half_index, True)
    expert_grad = grad_table[place_row].reshape(tok_count, top_count, feat_width)
    token_grad = jnp.sum(expert_grad.astype(jnp.float32), axis=1).astype(jnp.bfloat16)
    return (layer_out, token_grad, route_grad, gate_grad[None], up_grad[None], down_grad[None])


def expert_kernel(
    planes, tok_count, width, half, experts, tile,
    tok_ref, ids_ref, rw_ref, og_ref, wg_hbm, wu_hbm, wd_hbm,
    lo_ref, tg_ref, rg_ref, gg_ref, ug_ref, dg_ref,
    rows, parts, swapped, summed, first_a, first_b, turn_a, turn_b, second_a, second_b,
    zsend, zrecv, zown, hidden_all, pre_all, wg_ref, wu_ref, wd_ref,
    gg_buf, ug_buf, dg_buf, grad_sem, load_sem, z_ss, z_rs, x_ss, x_rs, y_ss, y_rs, xh_ss, xh_rs, yh_ss, yh_rs,
    core_ss, core_rs, swap_ss, swap_rs, fa_ss, fa_rs, fb_ss, fb_rs,
    ta_ss, ta_rs, tb_ss, tb_rs, zo_ss, zo_rs,
):
    f32, bf16 = jnp.float32, jnp.bfloat16
    dp, ex = lax.axis_index("dp"), lax.axis_index("expert")
    z, y, x, c = dp // 2, dp % 2, ex // 2, ex % 2
    piece = dp * lax.axis_size("expert") + ex
    mine = piece // 2
    full = 2 * width + LANES
    x_dev, y_dev, core_dev = (dp, (1 - x) * 2 + c), (z * 2 + 1 - y, ex), (dp, x * 2 + 1 - c)
    here, over_x, over_y, over_xy = y * 2 + x, y * 2 + 1 - x, (1 - y) * 2 + x, (1 - y) * 2 + 1 - x
    left, right = pl.ds(0, width), pl.ds(width, width + LANES)

    def remote(src, dst, send, recv, device):
        return pltpu.make_async_remote_copy(
            src_ref=src, dst_ref=dst, send_sem=send, recv_sem=recv,
            device_id=device, device_id_type=pl.DeviceIdType.MESH,
        )

    def landed(dst, send, recv):
        remote(dst, dst, send, recv, core_dev).wait_recv()

    def plane(step):
        reach = jnp.minimum(z, planes - 1 - z)
        away = (step + 1) // 2
        near = jnp.where(step % 2 == 1, z - away, z + away)
        far = jnp.where(z < planes - 1 - z, step, planes - 1 - step)
        return jnp.where(step <= 2 * reach, near, far)

    def load(i):
        src = (wg_hbm, wu_hbm, wd_hbm)[i]
        dst = (wg_ref, wu_ref, wd_ref)[i]
        return pltpu.make_async_copy(src.at[0], dst, load_sem.at[i])

    for i in range(3):
        load(i).start()

    lane = lax.broadcasted_iota(jnp.int32, (tok_count, LANES), 1)
    ids, weights = ids_ref[...].T, rw_ref[...].T
    table = [jnp.zeros((tok_count, LANES), f32) for _ in range(3)]
    for k in range(ids.shape[1]):
        for part in range(3):
            hit = lane == ids[:, k : k + 1] + part * experts
            table[part] = jnp.where(hit, weights[:, k : k + 1], table[part])
    head = table[0].astype(bf16).astype(f32)
    mid = table[1] - table[1].astype(bf16).astype(f32)
    mid = mid.astype(bf16).astype(f32)
    rest = table[2] - table[2].astype(bf16).astype(f32)
    rest = rest - rest.astype(bf16).astype(f32)
    rows[z, c, here, :, pl.ds(0, width)] = tok_ref[...]
    rows[z, c, here, :, pl.ds(width, width)] = og_ref[...]
    rows[z, c, here, :, pl.ds(2 * width, LANES)] = (head + mid + rest).astype(bf16)

    barrier = pltpu.get_barrier_semaphore()
    peers = [x_dev, y_dev, core_dev]
    peers += [(((z + d) % planes) * 2 + y, ex) for d in range(1, planes)]
    for peer in peers:
        pl.semaphore_signal(barrier, inc=1, device_id=peer, device_id_type=pl.DeviceIdType.MESH)
    pl.semaphore_wait(barrier, len(peers))

    def z_copy(q, way):
        slot = rows.at[q, c, here]
        peer = ((z + 1 - 2 * way) * 2 + y, ex)
        return remote(slot, slot, z_ss.at[q, way], z_rs.at[q], peer)

    def relay(q, run):
        @pl.when((q <= z) & (z < planes - 1))
        def _():
            run(z_copy(q, 0))

        @pl.when((q >= z) & (z > 0))
        def _():
            run(z_copy(q, 1))

    def x_copy(s):
        slot = rows.at[plane(s), c, here]
        return remote(slot, slot, x_ss.at[s], x_rs.at[s], x_dev)

    def y_copy(s):
        slot = rows.at[plane(s), c, here]
        return remote(slot, slot, y_ss.at[s], y_rs.at[s], y_dev)

    def xh_copy(s):
        slot = rows.at[plane(s), c, over_y, :, left]
        return remote(slot, slot, xh_ss.at[s], xh_rs.at[s], x_dev)

    def yh_copy(s):
        slot = rows.at[plane(s), c, over_x, :, right]
        return remote(slot, slot, yh_ss.at[s], yh_rs.at[s], y_dev)

    def core_copy(s, which):
        slot = rows.at[plane(s), c, (here, over_x, over_y, over_xy)[which]]
        return remote(slot, slot, core_ss.at[s, which], core_rs.at[s, which], core_dev)

    def swap_copy(s):
        q = plane(s)
        return remote(parts.at[q, 1 - c], swapped.at[q], swap_ss.at[s], swap_rs.at[s], core_dev)

    def fa_copy(s, to_y):
        src = summed.at[plane(s), to_y * 2 + 1 - x, :, left]
        return remote(src, first_a.at[s, to_y], fa_ss.at[s, to_y], fa_rs.at[s, to_y], x_dev)

    def fb_copy(s, to_x):
        src = summed.at[plane(s), (1 - y) * 2 + to_x, :, right]
        return remote(src, first_b.at[s, to_x], fb_ss.at[s, to_x], fb_rs.at[s, to_x], y_dev)

    def ta_copy(s):
        return remote(turn_a.at[s], second_a.at[s], ta_ss.at[s], ta_rs.at[s], y_dev)

    def tb_copy(s):
        return remote(turn_b.at[s], second_b.at[s], tb_ss.at[s], tb_rs.at[s], x_dev)

    def zo_copy(s):
        peer = (plane(s) * 2 + y, ex)
        return remote(zsend.at[s - 1], zrecv.at[z], zo_ss.at[s - 1], zo_rs.at[z], peer)

    def gather_one(s):
        @pl.when(s > 0)
        def _():
            landed(rows.at[plane(s), c, here], z_ss.at[plane(s), 0], z_rs.at[plane(s)])

        relay(plane(s), lambda copy: copy.start())
        x_copy(s).start()
        y_copy(s).start()
        core_copy(s, 0).start()

    def gather_two(s):
        q = plane(s)
        landed(rows.at[q, c, over_x], x_ss.at[s], x_rs.at[s])
        yh_copy(s).start()
        core_copy(s, 1).start()
        landed(rows.at[q, c, over_y], y_ss.at[s], y_rs.at[s])
        xh_copy(s).start()
        core_copy(s, 2).start()

    def gather_three(s):
        q = plane(s)
        landed(rows.at[q, c, over_xy, :, left], xh_ss.at[s], xh_rs.at[s])
        landed(rows.at[q, c, over_xy, :, right], yh_ss.at[s], yh_rs.at[s])
        core_copy(s, 3).start()

    group = 8 * tok_count
    glane = lax.broadcasted_iota(jnp.int32, (group, LANES), 1)

    def compute(s):
        q = plane(s)
        for which, slot in enumerate((here, over_x, over_y, over_xy)):
            landed(rows.at[q, 1 - c, slot], core_ss.at[s, which], core_rs.at[s, which])
        x_in = rows[q, :, :, :, 0:width].reshape(group, width)
        g_in = rows[q, :, :, :, width : 2 * width].reshape(group, width)
        gate = contract(x_in, wg_ref[...], 1, 0)
        up = contract(x_in, wu_ref[...], 1, 0)
        back = contract(g_in, wd_ref[...], 1, 1)
        tab = rows[q, :, :, :, 2 * width : full].reshape(group, LANES).astype(f32)
        own = (glane == mine) | (glane == mine + experts) | (glane == mine + 2 * experts)
        weight = jnp.sum(jnp.where(own, tab, 0.0), axis=1, keepdims=True)
        sig = 1.0 / (1.0 + jnp.exp(-gate))
        act = gate * sig
        hidden = act * up
        route = jnp.sum(hidden * back, axis=1, keepdims=True)
        coarse = route.astype(bf16).astype(f32)
        fine = route - coarse
        marks = jnp.where(glane == piece, coarse, jnp.where(glane == piece + LANES // 2, fine, 0.0))
        back = weight * back
        hid = (weight * hidden).astype(bf16)
        gate_pre = (back * up * sig * (1.0 + gate * (1.0 - sig))).astype(bf16)
        up_pre = (back * act).astype(bf16)
        at = pl.ds(pl.multiple_of(q * group, group), group)
        hidden_all[at, :] = hid
        pre_all[at, 0:half] = gate_pre
        pre_all[at, half : 2 * half] = up_pre
        shape = (2, 4, tok_count)
        for n in range(0, width, 2 * tile):
            cols = slice(n, n + 2 * tile)
            out = contract(hid, wd_ref[:, cols], 1, 0)
            parts[q, :, :, :, cols] = out.astype(bf16).reshape(shape + (2 * tile,))
            grad = contract(gate_pre, wg_ref[cols, :], 1, 1) + contract(up_pre, wu_ref[cols, :], 1, 1)
            after = slice(width + n, width + n + 2 * tile)
            parts[q, :, :, :, after] = grad.astype(bf16).reshape(shape + (2 * tile,))
        parts[q, :, :, :, 2 * width : full] = marks.astype(bf16).reshape(shape + (LANES,))
        swap_copy(s).start()

    def reduce_one(s):
        q = plane(s)
        landed(swapped.at[q], swap_ss.at[s], swap_rs.at[s])

        def add(t, carry):
            total = parts[q, c, t].astype(f32) + swapped[q, t].astype(f32)
            summed[q, t] = total.astype(bf16)
            return carry

        lax.fori_loop(0, 4, add, 0)
        fa_copy(s, 1 - y).start()
        fb_copy(s, 1 - x).start()
        fa_copy(s, y).start()
        fb_copy(s, x).start()

    def reduce_two(s):
        q = plane(s)
        landed(first_a.at[s, 1 - y], fa_ss.at[s, 1 - y], fa_rs.at[s, 1 - y])
        total = summed[q, over_y, :, 0:width].astype(f32) + first_a[s, 1 - y].astype(f32)
        turn_a[s] = total.astype(bf16)
        ta_copy(s).start()
        landed(first_b.at[s, 1 - x], fb_ss.at[s, 1 - x], fb_rs.at[s, 1 - x])
        total = summed[q, over_x, :, width:full].astype(f32) + first_b[s, 1 - x].astype(f32)
        turn_b[s] = total.astype(bf16)
        tb_copy(s).start()

    def reduce_three(s):
        q = plane(s)
        landed(first_a.at[s, y], fa_ss.at[s, y], fa_rs.at[s, y])
        landed(first_b.at[s, x], fb_ss.at[s, x], fb_rs.at[s, x])
        landed(second_a.at[s], ta_ss.at[s], ta_rs.at[s])
        landed(second_b.at[s], tb_ss.at[s], tb_rs.at[s])
        total_a = summed[q, here, :, 0:width].astype(f32) + first_a[s, y].astype(f32)
        total_a = total_a + second_a[s].astype(f32)
        total_b = summed[q, here, :, width:full].astype(f32) + first_b[s, x].astype(f32)
        total_b = total_b + second_b[s].astype(f32)

        @pl.when(s == 0)
        def _():
            zown[:, 0:width] = total_a
            zown[:, width:full] = total_b

        @pl.when(s > 0)
        def _():
            zsend[s - 1, :, 0:width] = total_a.astype(bf16)
            zsend[s - 1, :, width:full] = total_b.astype(bf16)
            zo_copy(s).start()

    every = planes * group
    tiles = width // tile

    def grad_copy(t, i):
        cols = pl.ds(pl.multiple_of(t * tile, tile), tile)
        src = (gg_buf.at[cols, :], ug_buf.at[cols, :], dg_buf.at[:, cols])[i]
        dst = (gg_ref.at[0, cols, :], ug_ref.at[0, cols, :], dg_ref.at[0, :, cols])[i]
        return pltpu.make_async_copy(src, dst, grad_sem.at[t, i])

    def weight_grads(t, carry):
        cols = pl.ds(pl.multiple_of(t * tile, tile), tile)
        x_in = rows[:, :, :, :, cols].reshape(every, tile)
        after = pl.ds(pl.multiple_of(width + t * tile, tile), tile)
        g_in = rows[:, :, :, :, after].reshape(every, tile)
        both = contract(x_in, pre_all[...], 0, 0).astype(bf16)
        gg_buf[cols, :] = both[:, 0:half]
        ug_buf[cols, :] = both[:, half : 2 * half]
        dg_buf[:, cols] = contract(hidden_all[...], g_in, 0, 0).astype(bf16)
        for i in range(3):
            grad_copy(t, i).start()
        return carry

    def step(i, carry):
        def stage(at, run):
            @pl.when((i >= at) & (i < at + planes))
            def _():
                run(i - at)

        stage(0, gather_one)
        stage(1, gather_two)
        stage(2, gather_three)

        @pl.when(i == 3)
        def _():
            for j in range(3):
                load(j).wait()

        stage(3, compute)
        stage(4, reduce_one)
        stage(5, reduce_two)
        stage(6, reduce_three)

        @pl.when(i >= planes + 3)
        def _():
            j = i - (planes + 3)
            lax.fori_loop((j * tiles) // 3, ((j + 1) * tiles) // 3, weight_grads, 0)

        return carry

    lax.fori_loop(0, planes + 6, step, 0)

    total = zown[...]
    for s in range(1, planes):
        origin = (z + s) % planes
        landed(zrecv.at[origin], zo_ss.at[s - 1], zo_rs.at[origin])
        total = total + zrecv[origin].astype(f32)
    lo_ref[...] = total[:, 0:width].astype(bf16)
    tg_ref[...] = total[:, width : 2 * width].astype(bf16)
    marks = total[:, 2 * width : full]
    routes = jnp.zeros((tok_count, LANES), f32)
    for k in range(ids.shape[1]):
        base = 2 * ids[:, k : k + 1]
        hit = (lane == base) | (lane == base + 1)
        hit = hit | (lane == base + LANES // 2) | (lane == base + LANES // 2 + 1)
        value = jnp.sum(jnp.where(hit, marks, 0.0), axis=1, keepdims=True)
        routes = jnp.where(lane == k, value, routes)
    rg_ref[...] = routes.T[0 : ids.shape[1], :]

    def drain(s, carry):
        x_copy(s).wait_send()
        y_copy(s).wait_send()
        xh_copy(s).wait_send()
        yh_copy(s).wait_send()
        for which in range(4):
            core_copy(s, which).wait_send()
        swap_copy(s).wait_send()
        for to in range(2):
            fa_copy(s, to).wait_send()
            fb_copy(s, to).wait_send()
        ta_copy(s).wait_send()
        tb_copy(s).wait_send()

        @pl.when(s > 0)
        def _():
            zo_copy(s).wait_send()

        relay(plane(s), lambda copy: copy.wait_send())

        return carry

    lax.fori_loop(0, planes, drain, 0)

    def stored(t, carry):
        for i in range(3):
            grad_copy(t, i).wait()
        return carry

    lax.fori_loop(0, tiles, stored, 0)


def finish_kernel(
    lo_in, tg_in, rg_in, gg_in, ug_in, dg_in, lo_ref, tg_ref, rg_ref, gg_ref, ug_ref, dg_ref,
    gg_buf, ug_buf, dg_buf, in_sem, out_sem,
):
    trips = ((gg_in, gg_buf, gg_ref), (ug_in, ug_buf, ug_ref), (dg_in, dg_buf, dg_ref))

    def pair(i, j):
        src, buf, dst = trips[i]
        count = buf.shape[0] // PARTS
        at = pl.ds(j * count, count)
        into = pltpu.make_async_copy(src.at[0, at, :], buf.at[at, :], in_sem.at[i, j])
        return into, pltpu.make_async_copy(buf.at[at, :], dst.at[0, at, :], out_sem.at[i, j])

    order = [(i, j) for i in range(3) for j in range(PARTS)]
    for i, j in order:
        pair(i, j)[0].start()
    lo_ref[...] = lo_in[...]
    tg_ref[...] = tg_in[...]
    rg_ref[...] = rg_in[...]
    for i, j in order:
        pair(i, j)[0].wait()
        pair(i, j)[1].start()
    for i, j in order:
        pair(i, j)[1].wait()


def kernel_body(tokens, expert_ids, route_weight, out_grad, gate_weight, up_weight, down_weight):
    dp_size, ex_size = lax.axis_size("dp"), lax.axis_size("expert")
    planes, experts = dp_size // 2, dp_size * ex_size // 2
    tok_count, width = tokens.shape
    half = gate_weight.shape[2]
    tile = TILE
    full = 2 * width + LANES
    bf16, f32 = jnp.bfloat16, jnp.float32
    every = planes * 8 * tok_count
    dma = pltpu.SemaphoreType.DMA
    vmem = pl.BlockSpec(memory_space=pltpu.VMEM)
    hbm = pl.BlockSpec(memory_space=pl.ANY)
    shape = jax.ShapeDtypeStruct
    sems = [dma((width // tile, 3)), dma((3,)), dma((planes, 2)), dma((planes,))]
    sems += [dma((planes,)) for _ in range(8)]
    sems += [dma((planes, 4))] * 2 + [dma((planes,))] * 2 + [dma((planes, 2))] * 4
    sems += [dma((planes,))] * 4 + [dma((planes - 1,)), dma((planes,))]
    outs = pl.pallas_call(
        functools.partial(expert_kernel, planes, tok_count, width, half, experts, tile),
        out_shape=(
            shape(tokens.shape, bf16),
            shape(tokens.shape, bf16),
            shape(route_weight.shape[::-1], f32),
            shape(gate_weight.shape, bf16),
            shape(up_weight.shape, bf16),
            shape(down_weight.shape, bf16),
        ),
        in_specs=[vmem] * 4 + [hbm] * 3,
        out_specs=[vmem] * 3 + [hbm] * 3,
        scratch_shapes=[
            pltpu.VMEM((planes, 2, 4, tok_count, full), bf16),
            pltpu.VMEM((planes, 2, 4, tok_count, full), bf16),
            pltpu.VMEM((planes, 4, tok_count, full), bf16),
            pltpu.VMEM((planes, 4, tok_count, full), bf16),
            pltpu.VMEM((planes, 2, tok_count, width), bf16),
            pltpu.VMEM((planes, 2, tok_count, width + LANES), bf16),
            pltpu.VMEM((planes, tok_count, width), bf16),
            pltpu.VMEM((planes, tok_count, width + LANES), bf16),
            pltpu.VMEM((planes, tok_count, width), bf16),
            pltpu.VMEM((planes, tok_count, width + LANES), bf16),
            pltpu.VMEM((planes - 1, tok_count, full), bf16),
            pltpu.VMEM((planes, tok_count, full), bf16),
            pltpu.VMEM((tok_count, full), f32),
            pltpu.VMEM((every, half), bf16),
            pltpu.VMEM((every, 2 * half), bf16),
            pltpu.VMEM(gate_weight.shape[1:], bf16),
            pltpu.VMEM(up_weight.shape[1:], bf16),
            pltpu.VMEM(down_weight.shape[1:], bf16),
            pltpu.VMEM(gate_weight.shape[1:], bf16),
            pltpu.VMEM(up_weight.shape[1:], bf16),
            pltpu.VMEM(down_weight.shape[1:], bf16),
        ] + sems,
        compiler_params=pltpu.CompilerParams(
            collective_id=0, has_side_effects=True, vmem_limit_bytes=60 * 1024 * 1024
        ),
    )(tokens, expert_ids.T, route_weight.T, out_grad, gate_weight, up_weight, down_weight)
    lo, tg, rg, gg, ug, dg = pl.pallas_call(
        finish_kernel,
        out_shape=tuple(shape(o.shape, o.dtype) for o in outs),
        in_specs=[vmem] * 3 + [hbm] * 3,
        out_specs=[vmem] * 3 + [hbm] * 3,
        scratch_shapes=[
            pltpu.VMEM(gate_weight.shape[1:], bf16),
            pltpu.VMEM(up_weight.shape[1:], bf16),
            pltpu.VMEM(down_weight.shape[1:], bf16),
            dma((3, PARTS)),
            dma((3, PARTS)),
        ],
        compiler_params=pltpu.CompilerParams(vmem_limit_bytes=60 * 1024 * 1024),
    )(*outs)
    return lo, tg, rg.T, gg, ug, dg


def solution(mesh):
    in_specs = (
        P(("dp", "expert"), None),
        P(("dp", "expert"), None),
        P(("dp", "expert"), None),
        P(("dp", "expert"), None),
        P(("dp", "expert"), None, None),
        P(("dp", "expert"), None, None),
        P(("dp", "expert"), None, None),
    )
    out_specs = (
        P(("dp", "expert"), None),
        P(("dp", "expert"), None),
        P(("dp", "expert"), None),
        P(("dp", "expert"), None, None),
        P(("dp", "expert"), None, None),
        P(("dp", "expert"), None, None),
    )
    dp_size, ex_size = mesh.shape["dp"], mesh.shape["expert"]
    pieces = dp_size * ex_size

    def step(tokens, expert_ids, *rest):
        capacity = 2 * (tokens.shape[0] * expert_ids.shape[1] // (pieces // 2))
        fits = ex_size == 4 and dp_size >= 4 and dp_size % 2 == 0 and 3 * pieces // 2 <= LANES
        fits = fits and pieces <= LANES // 2 and tokens.shape[1] % (2 * TILE) == 0
        form = kernel_body if fits and capacity >= tokens.shape[0] else body
        return form(tokens, expert_ids, *rest)

    return jax.shard_map(step, mesh=mesh, in_specs=in_specs, out_specs=out_specs, check_vma=False)
```
